32 devices in a mesh: dp: 4 (over y, x), ctx: 8 (over z, core).
Axes of the slice: x: 2, y: 2, z: 4, core: 2. Of those that a mesh axis runs over, the one named last changes fastest.
Arguments:
- inputs: float32 [4, 1024, 1088], P('dp', 'ctx'), may hold values from -6 to 6
- out_grad: float32 [4, 1024, 1088], P('dp', 'ctx'), may hold values from -6 to 6
- pair_blocks: int32 [8, 2], replicated, may hold values from 0 to 15, as said below
- triple_weight: float32 [1088, 3264], P('ctx', 'dp')
- merge_weight: float32 [1088, 1088], P('ctx', 'dp'), may hold values from -0.75 to 0.75
- expand_weight: float32 [1088, 4352], P('ctx', 'dp'), may hold values from -0.1875 to 0.1875
- shrink_weight: float32 [4352, 1088], P('ctx', 'dp'), may hold values from -0.09375 to 0.09375
- vector_params: float32 [1088, 12], P('ctx', 'dp')
- triple_moment: float32 [1088, 3264], P('ctx', 'dp'), may hold values from -24 to 24
- merge_moment: float32 [1088, 1088], P('ctx', 'dp'), may hold values from -6 to 6
- expand_moment: float32 [1088, 4352], P('ctx', 'dp'), may hold values from -6 to 6
- shrink_moment: float32 [4352, 1088], P('ctx', 'dp'), may hold values from -6 to 6
- vector_moment: float32 [1088, 12], P('ctx', 'dp'), may hold values from -112 to 112
- triple_square: float32 [1088, 3264], P('ctx', 'dp'), may hold values from 24.576 to 245.76
- merge_square: float32 [1088, 1088], P('ctx', 'dp'), may hold values from 8.192 to 81.92
- expand_square: float32 [1088, 4352], P('ctx', 'dp'), may hold values from 8.192 to 81.92
- shrink_square: float32 [4352, 1088], P('ctx', 'dp'), may hold values from 8.192 to 81.92
- vector_square: float32 [1088, 12], P('ctx', 'dp'), may hold values from 204.8 to 2048
Outputs:
- block_output: float32 [4, 1024, 1088], P('dp', 'ctx')
- input_grad: float32 [4, 1024, 1088], P('dp', 'ctx')
- triple_grad: float32 [1088, 3264], P('ctx', 'dp')
- merge_grad: float32 [1088, 1088], P('ctx', 'dp')
- expand_grad: float32 [1088, 4352], P('ctx', 'dp')
- shrink_grad: float32 [4352, 1088], P('ctx', 'dp')
- vector_grad: float32 [1088, 12], P('ctx', 'dp')
- triple_new: float32 [1088, 3264], P('ctx', 'dp')
- merge_new: float32 [1088, 1088], P('ctx', 'dp')
- expand_new: float32 [1088, 4352], P('ctx', 'dp')
- shrink_new: float32 [4352, 1088], P('ctx', 'dp')
- vector_new: float32 [1088, 12], P('ctx', 'dp')
- triple_moment_new: float32 [1088, 3264], P('ctx', 'dp')
- merge_moment_new: float32 [1088, 1088], P('ctx', 'dp')
- expand_moment_new: float32 [1088, 4352], P('ctx', 'dp')
- shrink_moment_new: float32 [4352, 1088], P('ctx', 'dp')
- vector_moment_new: float32 [1088, 12], P('ctx', 'dp')
- triple_square_new: float32 [1088, 3264], P('ctx', 'dp')
- merge_square_new: float32 [1088, 1088], P('ctx', 'dp')
- expand_square_new: float32 [1088, 4352], P('ctx', 'dp')
- shrink_square_new: float32 [4352, 1088], P('ctx', 'dp')
- vector_square_new: float32 [1088, 12], P('ctx', 'dp')
The draws below stay inside these ranges and needn't reach their ends.
Inputs may be any that keep to these rules, and one draw needn't show every extreme that they name: `pair_blocks`: row c names the two blocks of 64 positions that stand in stored rows c * 2 * 64 onward: first a block p, then 2 * 8 - 1 - p; each of the 16 blocks is named once.
All inputs are finite; a program needn't handle non-finite values.
Results may differ from the reference program's by a relative error of at most 0.011.
Values may be sent and summed in bfloat16 or wider, within the bound.
A program may use at most 256 MiB of HBM per device.

```python
import math
import jax
import jax.numpy as jnp
from jax import lax

D = 1088
H = 17
HD = 64
FF = 4352
BLK = 64
PAIRS = 8
SEQ = 1024
SEQS = 4
TOKENS = 4096


def draw_pair_blocks(key, part):
    order = jax.random.permutation(key, PAIRS).astype(jnp.int32)
    return jnp.stack([order, 2 * PAIRS - 1 - order], axis=1).astype(jnp.int32)


def draw_triple_weight(key, part):
    return jax.random.normal(key, (D, 3 * D), jnp.float32) * D ** (-0.5)


def draw_vector_params(key, part):
    noise = jax.random.normal(key, (D, 12), jnp.float32) * 0.2
    columns = jnp.arange(12, dtype=jnp.int32)
    offset = jnp.where((columns == 0) | (columns == 5), 1.0, 0.0).astype(jnp.float32)
    return noise + offset[None, :]


def levels(rng, dims, split, low, high):
    def one(axis_at, shards_of):
        steps = jax.random.uniform(jax.random.fold_in(jax.random.fold_in(rng, 6), axis_at), (shards_of,), jnp.float32, low / len(split), high / len(split))
        return jnp.repeat(jnp.exp(steps), dims[axis_at] // shards_of).reshape((-1,) + (1,) * (len(dims) - axis_at - 1))

    loudness = one(*split[0])
    for cut in split[1:]:
        loudness = loudness * one(*cut)
    return loudness


def centred(own_key, extent, deviation, reach, cuts=(), kind=jnp.bfloat16):
    entries = jax.random.normal(own_key, extent, jnp.float32) * deviation
    if len(cuts) > 0:
        entries = levels(own_key, extent, cuts, -0.22, 0.18) * entries
    return jnp.clip(entries, min=-reach, max=reach).astype(kind)


def setup_inputs(seed: int = 0) -> dict:
    keys = jax.random.split(jax.random.key(seed), 19)
    return {
        "inputs": centred(keys[0], (SEQS, SEQ, D), 1.0, 6.0, ((0, 4), (1, 8)), jnp.float32),
        "out_grad": centred(keys[1], (SEQS, SEQ, D), 1.0, 6.0, ((0, 4), (1, 8)), jnp.float32),
        "pair_blocks": draw_pair_blocks(jax.random.fold_in(keys[18], 71), 0),
        "triple_weight": draw_triple_weight(jax.random.fold_in(keys[18], 71), 0),
        "merge_weight": centred(keys[4], (D, D), (max(1, D * 64 // SEQ)) ** -0.5, 0.75, ((0, 8), (1, 4)), jnp.float32),
        "expand_weight": centred(keys[5], (D, FF), D ** -0.5, 0.1875, ((0, 8), (1, 4)), jnp.float32),
        "shrink_weight": centred(keys[6], (FF, D), FF ** -0.5, 0.09375, ((0, 8), (1, 4)), jnp.float32),
        "vector_params": draw_vector_params(jax.random.fold_in(keys[18], 71), 0),
        "triple_moment": centred(keys[8], (D, 3 * D), (0.06 * TOKENS ** 0.5), 24.0, ((0, 8), (1, 4)), jnp.float32),
        "merge_moment": centred(keys[9], (D, D), (0.03 * TOKENS ** 0.5), 6.0, ((0, 8), (1, 4)), jnp.float32),
        "expand_moment": centred(keys[10], (D, FF), (0.03 * TOKENS ** 0.5), 6.0, ((0, 8), (1, 4)), jnp.float32),
        "shrink_moment": centred(keys[11], (FF, D), (0.03 * TOKENS ** 0.5), 6.0, ((0, 8), (1, 4)), jnp.float32),
        "vector_moment": centred(keys[12], (D, 12), (0.3 * TOKENS ** 0.5), 112.0, ((0, 8), (1, 4)), jnp.float32),
        "triple_square": jnp.clip(jnp.exp(math.log(245.76) - 2.3025851 * jax.random.uniform(keys[13], (D, 3 * D), jnp.float32) ** levels(keys[13], (D, 3 * D), ((0, 8), (1, 4)), -0.2, 0.2)), 24.576, 245.76),
        "merge_square": jnp.clip(jnp.exp(math.log(81.92) - 2.30258502 * jax.random.uniform(keys[14], (D, D), jnp.float32) ** levels(keys[14], (D, D), ((0, 8), (1, 4)), -0.2, 0.2)), 8.192, 81.92),
        "expand_square": jnp.clip(jnp.exp(math.log(81.92) - 2.30258502 * jax.random.uniform(keys[15], (D, FF), jnp.float32) ** levels(keys[15], (D, FF), ((0, 8), (1, 4)), -0.2, 0.2)), 8.192, 81.92),
        "shrink_square": jnp.clip(jnp.exp(math.log(81.92) - 2.30258502 * jax.random.uniform(keys[16], (FF, D), jnp.float32) ** levels(keys[16], (FF, D), ((0, 8), (1, 4)), -0.2, 0.2)), 8.192, 81.92),
        "vector_square": jnp.clip(jnp.exp(math.log(2048.0) - 2.3025851 * jax.random.uniform(keys[17], (D, 12), jnp.float32) ** levels(keys[17], (D, 12), ((0, 8), (1, 4)), -0.2, 0.2)), 204.8, 2048.0),
    }


norm_eps = 1e-05
beta_first = 0.9
beta_second = 0.95
learn_rate = 0.01
decay_rate = 0.1
adam_eps = 1e-08
adam_steps = 4
gelu_coef = 0.7978845608028654
masked_score = -1e+30

def layer_norm(values):
    center = lax.optimization_barrier(jnp.mean(values, axis=-1, keepdims=True))
    shifted = values - center
    inverse = lax.rsqrt(lax.optimization_barrier(jnp.mean(shifted * shifted, axis=-1, keepdims=True)) + norm_eps)
    return (shifted * inverse, inverse)

def norm_back(incoming, normed, inverse, gain_vec):
    scaled = incoming * gain_vec
    return inverse * (scaled - lax.optimization_barrier(jnp.mean(scaled, axis=-1, keepdims=True)) - normed * lax.optimization_barrier(jnp.mean(scaled * normed, axis=-1, keepdims=True)))

def gelu_value(values):
    inside = gelu_coef * (values + 0.044715 * values * values * values)
    return 0.5 * values * (1.0 + jnp.tanh(inside))

def gelu_slope(values):
    inside = gelu_coef * (values + 0.044715 * values * values * values)
    tangent = jnp.tanh(inside)
    return 0.5 * (1.0 + tangent) + 0.5 * values * (1.0 - tangent * tangent) * gelu_coef * (1.0 + 3.0 * 0.044715 * values * values)

def adam_update(weight, gradient, moment, square, decayed):
    moment_new = beta_first * moment + (1.0 - beta_first) * gradient
    square_new = beta_second * square + (1.0 - beta_second) * gradient * gradient
    first_fix = 1.0 - beta_first ** adam_steps
    second_fix = 1.0 - beta_second ** adam_steps
    direction = moment_new / first_fix / (jnp.sqrt(square_new / second_fix) + adam_eps)
    if decayed:
        direction = direction + decay_rate * weight
    return (weight - learn_rate * direction, moment_new, square_new)

def attend_forward(query_b, key_b, value_b, positions):
    block_rows = min(512, SEQ)
    keys_full = key_b.astype(jnp.float32).reshape(SEQ, H, HD)
    values_full = value_b.astype(jnp.float32).reshape(SEQ, H, HD)
    score_scale = HD ** (-0.5)

    def one_block(index):
        start = index * block_rows
        query_full = lax.dynamic_slice_in_dim(query_b, start, block_rows, 0).astype(jnp.float32).reshape(block_rows, H, HD)
        query_pos = lax.dynamic_slice_in_dim(positions, start, block_rows, 0)
        scores = jnp.einsum('qhd,khd->hqk', query_full, keys_full) * score_scale
        allowed = query_pos[:, None] >= positions[None, :]
        scores = jnp.where(allowed[None, :, :], scores, masked_score)
        row_max = lax.optimization_barrier(jnp.max(scores, axis=2, keepdims=True))
        log_total = row_max + jnp.log(lax.optimization_barrier(jnp.sum(jnp.exp(scores - row_max), axis=2, keepdims=True)))
        probs_b = jnp.exp(scores - log_total).astype(jnp.bfloat16)
        attended = jnp.einsum('hqk,khd->qhd', probs_b.astype(jnp.float32), values_full)
        return (attended.reshape(block_rows, D).astype(jnp.bfloat16), log_total[:, :, 0])
    blocks_out, log_totals = lax.map(one_block, jnp.arange(SEQ // block_rows, dtype=jnp.int32))
    return (blocks_out.reshape(SEQ, D), log_totals)

def attend_backward(query_b, key_b, value_b, attended_b, dattended_b, log_totals, positions):
    block_rows = min(512, SEQ)
    keys_full = key_b.astype(jnp.float32).reshape(SEQ, H, HD)
    values_full = value_b.astype(jnp.float32).reshape(SEQ, H, HD)
    score_scale = HD ** (-0.5)

    def one_block(carry, inputs_block):
        dkey_sum, dvalue_sum = carry
        index, log_total = inputs_block
        start = index * block_rows
        query_full = lax.dynamic_slice_in_dim(query_b, start, block_rows, 0).astype(jnp.float32).reshape(block_rows, H, HD)
        dout_full = lax.dynamic_slice_in_dim(dattended_b, start, block_rows, 0).astype(jnp.float32).reshape(block_rows, H, HD)
        out_full = lax.dynamic_slice_in_dim(attended_b, start, block_rows, 0).astype(jnp.float32).reshape(block_rows, H, HD)
        query_pos = lax.dynamic_slice_in_dim(positions, start, block_rows, 0)
        scores = jnp.einsum('qhd,khd->hqk', query_full, keys_full) * score_scale
        allowed = query_pos[:, None] >= positions[None, :]
        scores = jnp.where(allowed[None, :, :], scores, masked_score)
        probs = jnp.exp(scores - log_total[:, :, None])
        probs_b = probs.astype(jnp.bfloat16)
        delta = lax.optimization_barrier(jnp.sum(dout_full * out_full, axis=2)).transpose(1, 0)[:, :, None]
        dprobs = jnp.einsum('qhd,khd->hqk', dout_full, values_full)
        dscores_b = (probs * (dprobs - delta) * score_scale).astype(jnp.bfloat16)
        dscores_full = dscores_b.astype(jnp.float32)
        dquery = jnp.einsum('hqk,khd->qhd', dscores_full, keys_full).reshape(block_rows, D)
        dkey_sum = dkey_sum + jnp.einsum('hqk,qhd->khd', dscores_full, query_full)
        dvalue_sum = dvalue_sum + jnp.einsum('hqk,qhd->khd', probs_b.astype(jnp.float32), dout_full)
        return ((dkey_sum, dvalue_sum), dquery)
    empty = jnp.zeros((SEQ, H, HD), jnp.float32)
    indices = jnp.arange(SEQ // block_rows, dtype=jnp.int32)
    (dkey_sum, dvalue_sum), dquery_blocks = lax.scan(one_block, (empty, empty), (indices, log_totals))
    return (dquery_blocks.reshape(SEQ, D), dkey_sum.reshape(SEQ, D), dvalue_sum.reshape(SEQ, D))

def one_sequence(stream, cotangent, positions, copies):
    w_triple, w_merge, w_expand, w_shrink, w_vector = copies
    vectors = w_vector.astype(jnp.float32)
    gain_one = vectors[:, 0]
    shift_one = vectors[:, 1]
    query_bias = vectors[:, 2]
    value_bias = vectors[:, 3]
    merge_bias = vectors[:, 4]
    gain_two = vectors[:, 5]
    shift_two = vectors[:, 6]
    shrink_bias = vectors[:, 7]
    expand_bias = vectors[:, 8:12].T.reshape(-1)
    normed_one, inverse_one = layer_norm(stream)
    act_one = (normed_one * gain_one + shift_one).astype(jnp.bfloat16)
    triple = jnp.dot(act_one, w_triple, preferred_element_type=jnp.float32)
    query_b = (triple[:, :D] + query_bias).astype(jnp.bfloat16)
    key_b = triple[:, D:2 * D].astype(jnp.bfloat16)
    value_b = (triple[:, 2 * D:] + value_bias).astype(jnp.bfloat16)
    attended_b, log_totals = attend_forward(query_b, key_b, value_b, positions)
    middle = stream + jnp.dot(attended_b, w_merge, preferred_element_type=jnp.float32) + merge_bias
    normed_two, inverse_two = layer_norm(middle)
    act_two = (normed_two * gain_two + shift_two).astype(jnp.bfloat16)
    pre_act = jnp.dot(act_two, w_expand, preferred_element_type=jnp.float32) + expand_bias
    hidden_b = gelu_value(pre_act).astype(jnp.bfloat16)
    block_out = middle + jnp.dot(hidden_b, w_shrink, preferred_element_type=jnp.float32) + shrink_bias
    cotangent_b = cotangent.astype(jnp.bfloat16)
    shrink_local = jnp.dot(hidden_b.T, cotangent_b, preferred_element_type=jnp.float32)
    shrink_bias_grad = lax.optimization_barrier(jnp.sum(cotangent, axis=0))
    dpre = jnp.dot(cotangent_b, w_shrink.T, preferred_element_type=jnp.float32) * gelu_slope(pre_act)
    dpre_b = dpre.astype(jnp.bfloat16)
    expand_local = jnp.dot(act_two.T, dpre_b, preferred_element_type=jnp.float32)
    expand_bias_grad = lax.optimization_barrier(jnp.sum(dpre, axis=0))
    dact_two = jnp.dot(dpre_b, w_expand.T, preferred_element_type=jnp.float32)
    gain_two_grad = lax.optimization_barrier(jnp.sum(dact_two * normed_two, axis=0))
    shift_two_grad = lax.optimization_barrier(jnp.sum(dact_two, axis=0))
    dmiddle = cotangent + norm_back(dact_two, normed_two, inverse_two, gain_two)
    dmiddle_b = dmiddle.astype(jnp.bfloat16)
    merge_local = jnp.dot(attended_b.T, dmiddle_b, preferred_element_type=jnp.float32)
    merge_bias_grad = lax.optimization_barrier(jnp.sum(dmiddle, axis=0))
    dattended_b = jnp.dot(dmiddle_b, w_merge.T, preferred_element_type=jnp.float32).astype(jnp.bfloat16)
    dquery, dkey, dvalue = attend_backward(query_b, key_b, value_b, attended_b, dattended_b, log_totals, positions)
    dtriple_b = jnp.concatenate([dquery, dkey, dvalue], axis=1).astype(jnp.bfloat16)
    triple_local = jnp.dot(act_one.T, dtriple_b, preferred_element_type=jnp.float32)
    query_bias_grad = lax.optimization_barrier(jnp.sum(dquery, axis=0))
    value_bias_grad = lax.optimization_barrier(jnp.sum(dvalue, axis=0))
    dact_one = jnp.dot(dtriple_b, w_triple.T, preferred_element_type=jnp.float32)
    gain_one_grad = lax.optimization_barrier(jnp.sum(dact_one * normed_one, axis=0))
    shift_one_grad = lax.optimization_barrier(jnp.sum(dact_one, axis=0))
    input_rows = dmiddle + norm_back(dact_one, normed_one, inverse_one, gain_one)
    vector_local = jnp.concatenate([jnp.stack([gain_one_grad, shift_one_grad, query_bias_grad, value_bias_grad, merge_bias_grad, gain_two_grad, shift_two_grad, shrink_bias_grad], axis=1), expand_bias_grad.reshape(4, D).T], axis=1)
    return (block_out, input_rows, (triple_local, merge_local, expand_local, shrink_local, vector_local))

def reference(inputs, out_grad, pair_blocks, triple_weight, merge_weight, expand_weight, shrink_weight, vector_params, triple_moment, merge_moment, expand_moment, shrink_moment, vector_moment, triple_square, merge_square, expand_square, shrink_square, vector_square):
    offsets = jnp.arange(BLK, dtype=jnp.int32)
    positions = (pair_blocks.reshape(-1)[:, None] * BLK + offsets[None, :]).reshape(-1).astype(jnp.int32)
    masters = (triple_weight, merge_weight, expand_weight, shrink_weight, vector_params)
    copies = tuple((master.astype(jnp.bfloat16) for master in masters))

    def per_sequence(totals, sequence_pair):
        stream, cotangent = sequence_pair
        block_out, input_rows, grads = one_sequence(stream, cotangent, positions, copies)
        return (tuple((running + grad_part for running, grad_part in zip(totals, grads))), (block_out, input_rows))
    zeros = tuple((jnp.zeros(master.shape, jnp.float32) for master in masters))
    totals, (block_output, input_grad) = lax.scan(per_sequence, zeros, (inputs, out_grad))
    moments = (triple_moment, merge_moment, expand_moment, shrink_moment, vector_moment)
    squares = (triple_square, merge_square, expand_square, shrink_square, vector_square)
    updated = [adam_update(masters[number], totals[number], moments[number], squares[number], number < 4) for number in range(5)]
    return (block_output, input_grad, totals[0], totals[1], totals[2], totals[3], totals[4], updated[0][0], updated[1][0], updated[2][0], updated[3][0], updated[4][0], updated[0][1], updated[1][1], updated[2][1], updated[3][1], updated[4][1], updated[0][2], updated[1][2], updated[2][2], updated[3][2], updated[4][2])
```

```python
import jax
import jax.numpy as jnp
from jax import lax
from jax.experimental import pallas as pl
from jax.experimental.pallas import tpu as pltpu
from jax.sharding import PartitionSpec as P

D = 1088
H = 17
HD = 64
BLK = 64


norm_eps = 1e-05
beta_first = 0.9
beta_second = 0.95
learn_rate = 0.01
decay_rate = 0.1
adam_eps = 1e-08
adam_steps = 4
gelu_coef = 0.7978845608028654
masked_score = -1e30


def layer_norm(values):
    center = jnp.mean(values, axis=-1, keepdims=True)
    shifted = values - center
    inverse = lax.rsqrt(jnp.mean(shifted * shifted, axis=-1, keepdims=True) + norm_eps)
    return (shifted * inverse, inverse)


def norm_back(incoming, normed, inverse, gain_vec):
    scaled = incoming * gain_vec
    return inverse * (
        scaled
        - jnp.mean(scaled, axis=-1, keepdims=True)
        - normed * jnp.mean(scaled * normed, axis=-1, keepdims=True)
    )


def gelu_value(values):
    inside = gelu_coef * (values + 0.044715 * values * values * values)
    return 0.5 * values * (1.0 + jnp.tanh(inside))


def gelu_slope(values):
    inside = gelu_coef * (values + 0.044715 * values * values * values)
    tangent = jnp.tanh(inside)
    return 0.5 * (1.0 + tangent) + 0.5 * values * (1.0 - tangent * tangent) * gelu_coef * (
        1.0 + 3.0 * 0.044715 * values * values
    )


def adam_update(weight, gradient, moment, square, decayed):
    moment_new = beta_first * moment + (1.0 - beta_first) * gradient
    square_new = beta_second * square + (1.0 - beta_second) * gradient * gradient
    first_fix = 1.0 - beta_first**adam_steps
    second_fix = 1.0 - beta_second**adam_steps
    direction = moment_new / first_fix / (jnp.sqrt(square_new / second_fix) + adam_eps)
    if decayed:
        direction = direction + decay_rate * weight
    return (weight - learn_rate * direction, moment_new, square_new)


def dot_on(left, right, left_dim, right_dim):
    return lax.dot_general(
        left, right, (((left_dim,), (right_dim,)), ((), ())), preferred_element_type=jnp.float32
    )


def head_probs(query_t, key_t, allowed):
    scores = dot_on(query_t, key_t, 0, 0) * HD ** (-0.5)
    scores = jnp.where(allowed, scores, masked_score)
    row_max = jnp.max(scores, axis=1, keepdims=True)
    weights = jnp.exp(scores - row_max)
    return weights / jnp.sum(weights, axis=1, keepdims=True)


def forward_kernel(query_pos, key_pos, query_ref, key_ref, value_ref, out_ref):
    allowed = query_pos[...] >= key_pos[...]
    probs = head_probs(query_ref[...], key_ref[...], allowed).astype(jnp.bfloat16)
    out_ref[...] = dot_on(value_ref[...], probs, 1, 1).astype(jnp.bfloat16)


def backward_kernel(
    query_pos, key_pos, query_ref, key_ref, value_ref, out_ref, dout_ref, dquery, dkey, dvalue
):
    allowed = query_pos[...] >= key_pos[...]
    query_t = query_ref[...]
    key_t = key_ref[...]
    dout_t = dout_ref[...]
    probs = head_probs(query_t, key_t, allowed)
    dprobs = dot_on(dout_t, value_ref[...], 0, 0)
    products = dout_t.astype(jnp.float32) * out_ref[...].astype(jnp.float32)
    delta = jnp.sum(products.T, axis=1, keepdims=True)
    dscores = (probs * (dprobs - delta) * HD ** (-0.5)).astype(jnp.bfloat16)
    dquery[...] = dot_on(key_t, dscores, 1, 1).astype(jnp.bfloat16)
    dkey[...] = dot_on(query_t, dscores, 1, 0).astype(jnp.bfloat16)
    dvalue[...] = dot_on(dout_t, probs.astype(jnp.bfloat16), 1, 0).astype(jnp.bfloat16)


def attention(kernel, query_pos, key_pos, features, out_rows):
    queries, keys = query_pos.shape[0], key_pos.shape[1]
    whole = lambda array: pl.BlockSpec(array.shape, lambda h: (0, 0))
    block = lambda width: pl.BlockSpec((HD, width), lambda h: (h, 0))
    shapes = [jax.ShapeDtypeStruct((H * HD, width), jnp.bfloat16) for width in out_rows]
    flops = 2 * H * HD * queries * keys * (2 if len(out_rows) == 1 else 5)
    return pl.pallas_call(
        kernel,
        grid=(H,),
        in_specs=[whole(query_pos), whole(key_pos)] + [block(x.shape[1]) for x in features],
        out_specs=[block(width) for width in out_rows],
        out_shape=shapes,
        cost_estimate=pl.CostEstimate(
            flops=flops, bytes_accessed=8 * H * HD * keys, transcendentals=H * queries * keys
        ),
    )(query_pos, key_pos, *features)


def exchange(blocks):
    return lax.all_to_all(blocks, "ctx", split_axis=0, concat_axis=0, tiled=True)


def scatter_rows(partial):
    return lax.psum_scatter(
        partial.astype(jnp.bfloat16), "ctx", scatter_dimension=0, tiled=True
    ).astype(jnp.float32)


def gather_rows(rows):
    return lax.all_gather(rows, "ctx", axis=0, tiled=True)


def local_wide(
    inputs,
    out_grad,
    pair_blocks,
    triple_weight,
    merge_weight,
    expand_weight,
    shrink_weight,
    vector_params,
    triple_moment,
    merge_moment,
    expand_moment,
    shrink_moment,
    vector_moment,
    triple_square,
    merge_square,
    expand_square,
    shrink_square,
    vector_square,
):
    bf16 = jnp.bfloat16
    n = lax.axis_size("ctx")
    m = lax.axis_size("dp")
    here = lax.axis_index("ctx")
    rows = inputs.shape[1]
    total = rows * n
    feat = D // n
    hidden_width = m * expand_weight.shape[1]
    wide = hidden_width // n
    stream = inputs[0]
    cotangent = out_grad[0]
    offsets = jnp.arange(BLK, dtype=jnp.int32)
    positions = (pair_blocks.reshape(-1)[:, None] * BLK + offsets[None, :]).reshape(-1)
    query_pos = lax.dynamic_slice_in_dim(positions, here * rows, rows)[:, None]
    key_pos = positions[None, :]

    packed = jnp.concatenate(
        [
            triple_weight.astype(bf16),
            merge_weight.astype(bf16),
            expand_weight.astype(bf16),
            vector_params.astype(bf16),
        ],
        axis=1,
    )
    tw, mw, ew = triple_weight.shape[1], merge_weight.shape[1], expand_weight.shape[1]
    columns = lax.all_gather(packed, "dp", axis=0)

    def take(start, width):
        return columns[:, :, start : start + width].transpose(1, 0, 2).reshape(feat, m * width)

    triple_rows = take(0, tw)
    merge_rows = take(tw, mw)
    expand_rows = take(tw + mw, ew)
    vector_rows = take(tw + mw + ew, vector_params.shape[1])
    normed_one, inverse_one = layer_norm(stream)
    normed_full = gather_rows(normed_one.astype(bf16))
    send = jnp.concatenate(
        [
            triple_rows.reshape(feat, 3, n, feat).transpose(2, 0, 1, 3).reshape(n, feat, 3 * feat),
            expand_rows.reshape(feat, n, wide).transpose(1, 0, 2),
        ],
        axis=2,
    )
    got = exchange(send).reshape(D, 3 * feat + wide)
    w_triple = got[:, : 3 * feat]
    w_expand = got[:, 3 * feat :]
    merged = gather_rows(jnp.concatenate([merge_rows, vector_rows], axis=1))
    w_merge = merged[:, :D]
    vectors = merged[:, D:].astype(jnp.float32)
    gain_one = vectors[:, 0]
    shift_one = vectors[:, 1]
    query_bias = lax.dynamic_slice_in_dim(vectors[:, 2], here * feat, feat)
    value_bias = lax.dynamic_slice_in_dim(vectors[:, 3], here * feat, feat)
    merge_bias = vectors[:, 4]
    gain_two = vectors[:, 5]
    shift_two = vectors[:, 6]
    shrink_bias = vectors[:, 7]
    expand_bias = lax.dynamic_slice_in_dim(vectors[:, 8:].T.reshape(-1), here * wide, wide)

    act_one = (normed_full.astype(jnp.float32) * gain_one + shift_one).astype(bf16)
    bias = jnp.concatenate([query_bias, jnp.zeros_like(query_bias), value_bias])
    triple_t = (dot_on(w_triple, act_one, 0, 1) + bias[:, None]).astype(bf16)
    query_t = exchange(triple_t[:feat].reshape(feat, n, rows).transpose(1, 0, 2)).reshape(D, rows)
    both = lax.all_gather(triple_t[feat:].reshape(2, feat, total), "ctx", axis=0)
    key_t = both[:, 0].reshape(D, total)
    value_t = both[:, 1].reshape(D, total)
    (attended_t,) = attention(
        forward_kernel, query_pos, key_pos, (query_t, key_t, value_t), (rows,)
    )
    cot_full = gather_rows(cotangent.astype(bf16))
    w_shrink = (
        lax.all_gather(shrink_weight.astype(bf16), "dp", axis=0).transpose(1, 0, 2).reshape(wide, D)
    )
    middle = stream + dot_on(attended_t, w_merge, 0, 0) + merge_bias
    normed_two, inverse_two = layer_norm(middle)
    act_two = gather_rows((normed_two * gain_two + shift_two).astype(bf16))
    pre_act = dot_on(act_two, w_expand, 1, 0) + expand_bias
    hidden_b = gelu_value(pre_act).astype(bf16)
    dpre = dot_on(cot_full, w_shrink, 1, 1) * gelu_slope(pre_act)
    dpre_b = dpre.astype(bf16)
    expand_bias_grad = jnp.sum(dpre, axis=0)
    dact_two = scatter_rows(dot_on(dpre_b, w_expand, 1, 1))
    block_out = middle + scatter_rows(dot_on(hidden_b, w_shrink, 1, 0)) + shrink_bias
    shrink_part = dot_on(hidden_b, cot_full, 0, 0).astype(bf16)
    expand_part = dot_on(act_two, dpre_b, 0, 0).astype(bf16)
    shrink_grad = lax.psum_scatter(
        shrink_part.reshape(wide, m, D // m).transpose(1, 0, 2), "dp", scatter_dimension=0
    ).astype(jnp.float32)
    shrink_bias_grad = jnp.sum(cotangent, axis=0)
    gain_two_grad = jnp.sum(dact_two * normed_two, axis=0)
    shift_two_grad = jnp.sum(dact_two, axis=0)
    dmiddle = cotangent + norm_back(dact_two, normed_two, inverse_two, gain_two)
    dmiddle_b = dmiddle.astype(bf16)
    merge_part = lax.psum_scatter(
        dot_on(attended_t, dmiddle_b, 1, 0).astype(bf16), "ctx", scatter_dimension=0, tiled=True
    )
    merge_bias_grad = jnp.sum(dmiddle, axis=0)
    dattended_t = dot_on(w_merge, dmiddle_b, 1, 1).astype(bf16)
    dquery_t, dkey_t, dvalue_t = attention(
        backward_kernel,
        query_pos,
        key_pos,
        (query_t, key_t, value_t, attended_t, dattended_t),
        (rows, total, total),
    )
    dquery_c = exchange(dquery_t.reshape(n, feat, rows)).transpose(1, 0, 2).reshape(feat, total)
    dkey_c = lax.psum_scatter(dkey_t, "ctx", scatter_dimension=0, tiled=True)
    dvalue_c = lax.psum_scatter(dvalue_t, "ctx", scatter_dimension=0, tiled=True)
    dtriple_t = jnp.concatenate([dquery_c, dkey_c, dvalue_c], axis=0)
    query_bias_grad = jnp.sum(dquery_c.astype(jnp.float32), axis=1)
    value_bias_grad = jnp.sum(dvalue_c.astype(jnp.float32), axis=1)
    dact_one = scatter_rows(dot_on(dtriple_t, w_triple, 0, 1))
    triple_part = dot_on(act_one, dtriple_t, 0, 1).astype(bf16)
    gain_one_grad = jnp.sum(dact_one * normed_one, axis=0)
    shift_one_grad = jnp.sum(dact_one, axis=0)
    input_rows = dmiddle + norm_back(dact_one, normed_one, inverse_one, gain_one)

    def place(piece, size):
        return lax.dynamic_update_slice_in_dim(
            jnp.zeros((size,), jnp.float32), piece, here * piece.shape[0], 0
        )

    vector_local = jnp.concatenate(
        [
            jnp.stack(
                [
                    gain_one_grad,
                    shift_one_grad,
                    place(query_bias_grad, D),
                    place(value_bias_grad, D),
                    merge_bias_grad,
                    gain_two_grad,
                    shift_two_grad,
                    shrink_bias_grad,
                ],
                axis=1,
            ),
            place(expand_bias_grad, hidden_width).reshape(-1, D).T,
        ],
        axis=1,
    )
    vector_part = lax.psum_scatter(vector_local, "ctx", scatter_dimension=0, tiled=True)

    def by_dp(rows_part):
        return rows_part.reshape(feat, m, -1).transpose(1, 0, 2)

    expand_rows_part = exchange(expand_part.reshape(n, feat, wide)).transpose(1, 0, 2)
    expand_grad = lax.psum_scatter(by_dp(expand_rows_part), "dp", scatter_dimension=0).astype(
        jnp.float32
    )
    triple_rows_part = (
        exchange(triple_part.reshape(n, feat, 3 * feat))
        .reshape(n, feat, 3, feat)
        .transpose(1, 2, 0, 3)
    )
    last = lax.psum_scatter(
        jnp.concatenate(
            [by_dp(triple_rows_part), by_dp(merge_part), by_dp(vector_part).astype(bf16)], axis=2
        ),
        "dp",
        scatter_dimension=0,
    ).astype(jnp.float32)
    triple_grad = last[:, :tw]
    merge_grad = last[:, tw : tw + mw]
    vector_grad = last[:, tw + mw :]
    triple_new, triple_moment_new, triple_square_new = adam_update(
        triple_weight, triple_grad, triple_moment, triple_square, True
    )
    merge_new, merge_moment_new, merge_square_new = adam_update(
        merge_weight, merge_grad, merge_moment, merge_square, True
    )
    expand_new, expand_moment_new, expand_square_new = adam_update(
        expand_weight, expand_grad, expand_moment, expand_square, True
    )
    shrink_new, shrink_moment_new, shrink_square_new = adam_update(
        shrink_weight, shrink_grad, shrink_moment, shrink_square, True
    )
    vector_new, vector_moment_new, vector_square_new = adam_update(
        vector_params, vector_grad, vector_moment, vector_square, False
    )
    return (
        block_out[None],
        input_rows[None],
        triple_grad,
        merge_grad,
        expand_grad,
        shrink_grad,
        vector_grad,
        triple_new,
        merge_new,
        expand_new,
        shrink_new,
        vector_new,
        triple_moment_new,
        merge_moment_new,
        expand_moment_new,
        shrink_moment_new,
        vector_moment_new,
        triple_square_new,
        merge_square_new,
        expand_square_new,
        shrink_square_new,
        vector_square_new,
    )


TILE = 2 * HD


def peers_of(kinds):
    me_c = lax.axis_index("ctx")
    me_d = lax.axis_index("dp")
    n = lax.axis_size("ctx")
    m = lax.axis_size("dp")
    chips = n // 2
    chip = lax.div(me_c, 2)
    core = lax.rem(me_c, 2)
    found = []
    if any(kind.endswith("dp") for kind in kinds):
        found += [{"dp": lax.rem(me_d + r, m)} for r in range(1, m)]
    if "swap_ctx" in kinds:
        found += [{"ctx": lax.rem(me_c + r, n)} for r in range(1, n)]
    elif any(kind.endswith("ctx") for kind in kinds):
        found += [{"ctx": 2 * lax.rem(chip + r, chips) + core} for r in range(1, chips)]
        found += [{"ctx": 2 * chip + 1 - core}]
    return found


def send(src, dst, send_sem, recv_sem, device):
    return pltpu.make_async_remote_copy(
        src_ref=src,
        dst_ref=dst,
        send_sem=send_sem,
        recv_sem=recv_sem,
        device_id=device,
        device_id_type=pl.DeviceIdType.MESH,
    )


class GatherDp:
    scratch = 0

    def __init__(self, x, out, sems):
        self.x, self.out, self.sems = x, out, sems
        self.m = lax.axis_size("dp")
        self.me = lax.axis_index("dp")

    def piece(self, to):
        return self.x

    def target(self, of):
        return self.out.at[of]

    def copy(self, r, of, to):
        return send(
            self.piece(to),
            self.target(of),
            self.sems[0].at[r],
            self.sems[1].at[of],
            {"dp": to},
        )

    def start(self):
        self.sent = []
        for r in range(1, self.m):
            copy = self.copy(r, self.me, lax.rem(self.me + r, self.m))
            copy.start()
            self.sent.append(copy)
        self.keep()

    def keep(self):
        self.out[self.me] = self.x[...]

    def middle(self):
        pass

    def finish(self):
        for r in range(1, self.m):
            of = lax.rem(self.me + self.m - r, self.m)
            self.copy(r, of, of).wait_recv()
        for copy in self.sent:
            copy.wait_send()


class SwapDp(GatherDp):
    def piece(self, to):
        return self.x.at[to]

    def keep(self):
        self.out[self.me] = self.x[self.me]


class SumDp(SwapDp):
    scratch = 1

    def __init__(self, x, out, sems, got):
        super().__init__(x, out, sems)
        self.got = got

    def target(self, of):
        return self.got.at[of]

    def keep(self):
        pass

    def finish(self):
        super().finish()
        total = self.x[self.me].astype(jnp.float32)
        for r in range(1, self.m):
            total = total + self.got[lax.rem(self.me + r, self.m)].astype(jnp.float32)
        self.out[...] = total


class SwapCtx(SwapDp):
    def __init__(self, x, out, sems):
        self.x, self.out, self.sems = x, out, sems
        self.m = lax.axis_size("ctx")
        self.me = lax.axis_index("ctx")

    def copy(self, r, of, to):
        return send(
            self.piece(to),
            self.target(of),
            self.sems[0].at[r],
            self.sems[1].at[of],
            {"ctx": to},
        )


class GatherCtx:
    scratch = 0

    def __init__(self, x, out, sems):
        self.x, self.out, self.sems = x, out, sems
        self.chips = lax.axis_size("ctx") // 2
        self.me = lax.axis_index("ctx")
        self.chip = lax.div(self.me, 2)
        self.core = lax.rem(self.me, 2)
        self.partner = 2 * self.chip + 1 - self.core

    def of_chip(self, r, core):
        return 2 * lax.rem(self.chip + self.chips + r, self.chips) + core

    def copy(self, src, slot, of, to):
        return send(
            src, self.out.at[of], self.sems[0].at[slot], self.sems[1].at[of], {"ctx": to}
        )

    def start(self):
        self.sent = []
        for r in range(1, self.chips):
            copy = self.copy(self.x, r, self.me, self.of_chip(r, self.core))
            copy.start()
            self.sent.append(copy)
        copy = self.copy(self.x, 0, self.me, self.partner)
        copy.start()
        self.sent.append(copy)
        self.out[self.me] = self.x[...]

    def middle(self):
        for r in range(1, self.chips):
            of = self.of_chip(-r, self.core)
            self.copy(self.x, r, of, of).wait_recv()
            copy = self.copy(self.out.at[of], self.chips + r, of, self.partner)
            copy.start()
            self.sent.append(copy)

    def finish(self):
        for r in range(self.chips):
            of = self.of_chip(-r, 1 - self.core)
            self.copy(self.x, 0, of, self.partner).wait_recv()
        for copy in self.sent:
            copy.wait_send()


class SumCtx(GatherCtx):
    scratch = 3

    def __init__(self, x, out, sems, half, pre, got):
        super().__init__(x, out, sems)
        self.half, self.pre, self.got = half, pre, got

    def early(self, r):
        j = lax.rem(self.chip + r, self.chips)
        return send(
            self.x.at[2 * j + 1 - self.core],
            self.half.at[j],
            self.sems[0].at[r],
            self.sems[1].at[j],
            {"ctx": self.partner},
        )

    def late(self, r, of, to):
        return send(
            self.pre.at[to],
            self.got.at[of],
            self.sems[0].at[self.chips + r],
            self.sems[1].at[self.chips + of],
            {"ctx": 2 * to + self.core},
        )

    def start(self):
        self.sent = []
        for r in list(range(1, self.chips)) + [0]:
            copy = self.early(r)
            copy.start()
            self.sent.append(copy)

    def middle(self):
        for r in range(1, self.chips):
            self.early(r).wait_recv()
            to = lax.rem(self.chip + r, self.chips)
            total = self.x[2 * to + self.core].astype(jnp.float32) + self.half[to].astype(
                jnp.float32
            )
            self.pre[to] = total.astype(self.pre.dtype)
            copy = self.late(r, self.chip, to)
            copy.start()
            self.sent.append(copy)

    def finish(self):
        self.early(0).wait_recv()
        total = self.x[self.me].astype(jnp.float32) + self.half[self.chip].astype(jnp.float32)
        for r in range(1, self.chips):
            of = lax.rem(self.chip + self.chips - r, self.chips)
            self.late(r, of, of).wait_recv()
            total = total + self.got[of].astype(jnp.float32)
        self.out[...] = total
        for copy in self.sent:
            copy.wait_send()


MOVES = {
    "gather_dp": GatherDp,
    "swap_dp": SwapDp,
    "sum_dp": SumDp,
    "gather_ctx": GatherCtx,
    "swap_ctx": SwapCtx,
    "sum_ctx": SumCtx,
}


def move_kernel(kinds, *refs):
    count = len(kinds)
    xs, outs, rest = refs[:count], refs[count : 2 * count], list(refs[2 * count :])
    barrier = pltpu.get_barrier_semaphore()
    peers = peers_of(kinds)
    for peer in peers:
        pl.semaphore_signal(
            barrier, inc=1, device_id=peer, device_id_type=pl.DeviceIdType.MESH
        )
    pl.semaphore_wait(barrier, len(peers))
    moves = []
    for kind, x, out in zip(kinds, xs, outs):
        sems = (rest.pop(0), rest.pop(0))
        extra = [rest.pop(0) for _ in range(MOVES[kind].scratch)]
        moves.append(MOVES[kind](x, out, sems, *extra))
    for move in moves:
        move.start()
    for move in moves:
        move.middle()
    for move in moves:
        move.finish()


def move(collective_id, *pairs):
    kinds = tuple(kind for kind, _ in pairs)
    n = lax.axis_size("ctx")
    m = lax.axis_size("dp")
    shapes, scratch, sent = [], [], 0
    for kind, x in pairs:
        size = n if kind.endswith("ctx") else m
        if kind.startswith("gather"):
            shapes.append(jax.ShapeDtypeStruct((size,) + x.shape, x.dtype))
            sent += (size - 1) * x.size * x.dtype.itemsize
        elif kind.startswith("swap"):
            shapes.append(jax.ShapeDtypeStruct(x.shape, x.dtype))
            sent += x.size * x.dtype.itemsize
        else:
            shapes.append(jax.ShapeDtypeStruct(x.shape[1:], jnp.float32))
            sent += x.size * x.dtype.itemsize
        scratch += [pltpu.SemaphoreType.DMA((size,)), pltpu.SemaphoreType.DMA((size,))]
        if kind == "sum_dp":
            scratch += [pltpu.VMEM(x.shape, x.dtype)]
        if kind == "sum_ctx":
            scratch += [pltpu.VMEM((n // 2,) + x.shape[1:], x.dtype)] * 3
    kernel = lambda *refs: move_kernel(kinds, *refs)
    return pl.pallas_call(
        kernel,
        in_specs=[pl.BlockSpec(memory_space=pltpu.VMEM)] * len(kinds),
        out_specs=[pl.BlockSpec(memory_space=pltpu.VMEM)] * len(kinds),
        out_shape=shapes,
        scratch_shapes=scratch,
        compiler_params=pltpu.CompilerParams(
            collective_id=collective_id, has_side_effects=True
        ),
        cost_estimate=pl.CostEstimate(flops=sent * 100, bytes_accessed=sent, transcendentals=0),
        name="move_" + str(collective_id),
    )(*[x for _, x in pairs])


def pair_lanes(shape, half):
    lane = lax.broadcasted_iota(jnp.int32, shape, 1)
    return (lane < HD) if half == 0 else (lane >= HD)


def causal(shape):
    row = lax.broadcasted_iota(jnp.int32, shape, 0)
    return row >= lax.broadcasted_iota(jnp.int32, shape, 1)


def sort_rows(order_ref, src, dst):
    for b in range(src.shape[0] // BLK):
        start = pl.multiple_of(order_ref[b] * BLK, BLK)
        dst[b * BLK : (b + 1) * BLK, :] = src[pl.ds(start, BLK), :]


def unsort_rows(order_ref, src, dst):
    for b in range(dst.shape[0] // BLK):
        start = pl.multiple_of(order_ref[b] * BLK, BLK)
        dst[pl.ds(start, BLK), :] = src[b * BLK : (b + 1) * BLK, :]


def head_slots():
    return ((0, 0), (0, 1), (1, 0))


def pairs_forward(order_ref, qkv_ref, out_ref, log_ref, rows, outs):
    sort_rows(order_ref, qkv_ref, rows)
    seq = qkv_ref.shape[0]
    step = min(4 * BLK, seq)
    for i in range(seq // step):
        at = slice(i * step, (i + 1) * step)
        results, logs = [], []
        for block, half in head_slots():
            lanes = lambda part: slice((2 * part + block) * TILE, (2 * part + block + 1) * TILE)
            query = rows[at, lanes(0)] * HD ** (-0.5)
            query = query.astype(jnp.bfloat16)
            if block == 0:
                query = jnp.where(pair_lanes(query.shape, half), query, jnp.zeros_like(query))
            last = dot_on(query, rows[at, lanes(1)], 1, 1)
            last = jnp.where(causal(last.shape), last, masked_score)
            top = jnp.max(last, axis=1, keepdims=True)
            if i > 0:
                early = dot_on(query, rows[: i * step, lanes(1)], 1, 1)
                top = jnp.maximum(top, jnp.max(early, axis=1, keepdims=True))
            last = jnp.exp(last - top)
            total = jnp.sum(last, axis=1, keepdims=True)
            if i > 0:
                early = jnp.exp(early - top)
                total = total + jnp.sum(early, axis=1, keepdims=True)
            scale = 1.0 / total
            result = dot_on((last * scale).astype(jnp.bfloat16), rows[at, lanes(2)], 1, 0)
            if i > 0:
                result = result + dot_on(
                    (early * scale).astype(jnp.bfloat16), rows[: i * step, lanes(2)], 1, 0
                )
            results.append(result)
            logs.append(top + jnp.log(total))
        first = pair_lanes((step, TILE), 0)
        outs[at, :TILE] = jnp.where(first, results[0], results[1]).astype(jnp.bfloat16)
        outs[at, TILE:] = results[2].astype(jnp.bfloat16)
        lane = lax.broadcasted_iota(jnp.int32, (step, TILE), 1)
        log_ref[at, :] = jnp.where(lane == 0, logs[0], jnp.where(lane == 1, logs[1], logs[2]))
    unsort_rows(order_ref, outs, out_ref)


def pairs_backward(
    order_ref, qkv_ref, out_ref, log_ref, dout_ref, dqkv_ref, rows, outs, douts, grads, dkey, dvalue
):
    sort_rows(order_ref, qkv_ref, rows)
    sort_rows(order_ref, out_ref, outs)
    sort_rows(order_ref, dout_ref, douts)
    seq = qkv_ref.shape[0]
    step = min(4 * BLK, seq)
    dkey[...] = jnp.zeros_like(dkey)
    dvalue[...] = jnp.zeros_like(dvalue)
    for i in range(seq // step):
        at = slice(i * step, (i + 1) * step)
        dqueries = []
        for slot, (block, half) in enumerate(head_slots()):
            lanes = lambda part: slice((2 * part + block) * TILE, (2 * part + block + 1) * TILE)
            own = slice(block * TILE, (block + 1) * TILE)
            query = (rows[at, lanes(0)] * HD ** (-0.5)).astype(jnp.bfloat16)
            dout = douts[at, own]
            if block == 0:
                mask = pair_lanes(query.shape, half)
                query = jnp.where(mask, query, jnp.zeros_like(query))
                dout = jnp.where(mask, dout, jnp.zeros_like(dout))
            delta = jnp.sum(
                dout.astype(jnp.float32) * outs[at, own].astype(jnp.float32), axis=1, keepdims=True
            )
            log_total = log_ref[at, slot : slot + 1]
            dquery = None
            for keys, diagonal in ((at, True), (slice(0, i * step), False)):
                if keys.stop == 0:
                    continue
                scores = dot_on(query, rows[keys, lanes(1)], 1, 1)
                probs = jnp.exp(scores - log_total)
                if diagonal:
                    probs = jnp.where(causal(probs.shape), probs, 0.0)
                dprobs = dot_on(dout, rows[keys, lanes(2)], 1, 1)
                dscores = (probs * (dprobs - delta)).astype(jnp.bfloat16)
                part = dot_on(dscores, rows[keys, lanes(1)], 1, 0)
                dquery = part if dquery is None else dquery + part
                dkey[own, keys] += dot_on(query, dscores, 0, 0)
                dvalue[own, keys] += dot_on(dout, probs.astype(jnp.bfloat16), 0, 0)
            dqueries.append(dquery * HD ** (-0.5))
        first = pair_lanes((step, TILE), 0)
        grads[at, :TILE] = jnp.where(first, dqueries[0], dqueries[1]).astype(jnp.bfloat16)
        third = jnp.where(first, dqueries[2], 0.0)
        grads[at, TILE : 2 * TILE] = third.astype(jnp.bfloat16)
    for block in range(2):
        own = slice(block * TILE, (block + 1) * TILE)
        grads[:, (2 + block) * TILE : (3 + block) * TILE] = dkey[own, :].T.astype(jnp.bfloat16)
        grads[:, (4 + block) * TILE : (5 + block) * TILE] = dvalue[own, :].T.astype(jnp.bfloat16)
    unsort_rows(order_ref, grads, dqkv_ref)


def attend(kernel, order, arrays, shapes, scratch, matmuls):
    seq = arrays[0].shape[0]
    vmem = pl.BlockSpec(memory_space=pltpu.VMEM)
    return pl.pallas_call(
        kernel,
        in_specs=[pl.BlockSpec(memory_space=pltpu.SMEM)] + [vmem] * len(arrays),
        out_specs=[vmem] * len(shapes),
        out_shape=shapes,
        scratch_shapes=scratch,
        cost_estimate=pl.CostEstimate(
            flops=3 * matmuls * seq * seq * TILE,
            bytes_accessed=seq * 24 * TILE,
            transcendentals=2 * seq * seq,
        ),
    )(order, *arrays)


def turn(x, r):
    n = lax.axis_size("ctx")
    chips = n // 2
    pairs = [(2 * q + k, 2 * ((q + r) % chips) + k) for q in range(chips) for k in range(2)]
    return lax.ppermute(x, "ctx", pairs)


def trade(x):
    return lax.ppermute(x, "ctx", [(c, c ^ 1) for c in range(lax.axis_size("ctx"))])


def line_gather(x):
    chips = lax.axis_size("ctx") // 2
    chip = lax.axis_index("ctx") // 2
    out = jnp.zeros((chips,) + x.shape, x.dtype)
    for r in range(chips):
        piece = x if r == 0 else turn(x, r)
        out = lax.dynamic_update_index_in_dim(out, piece, (chip - r) % chips, 0)
    return out


def line_sum(x):
    chips = lax.axis_size("ctx") // 2
    chip = lax.axis_index("ctx") // 2
    total = lax.dynamic_index_in_dim(x, chip, 0, False).astype(jnp.float32)
    for r in range(1, chips):
        piece = lax.dynamic_index_in_dim(x, (chip + r) % chips, 0, False)
        total = total + turn(piece, r).astype(jnp.float32)
    return total


def both_cores(x, other, axis):
    core = lax.axis_index("ctx") % 2
    return jnp.where(core == 0, jnp.stack([x, other], axis), jnp.stack([other, x], axis))


def core_sum(x, axis):
    core = lax.axis_index("ctx") % 2
    mine = lax.dynamic_index_in_dim(x, core, axis, False)
    other = lax.dynamic_index_in_dim(x, 1 - core, axis, False)
    return (mine.astype(jnp.float32) + trade(other).astype(jnp.float32)).astype(x.dtype)


def swap_dp(x):
    m = lax.axis_size("dp")
    me = lax.axis_index("dp")
    out = jnp.zeros_like(x)
    for r in range(m):
        piece = lax.dynamic_index_in_dim(x, (me + r) % m, 0, False)
        if r:
            piece = lax.ppermute(piece, "dp", [(d, (d + r) % m) for d in range(m)])
        out = lax.dynamic_update_index_in_dim(out, piece, (me - r) % m, 0)
    return out


def local_pairs(
    inputs,
    out_grad,
    pair_blocks,
    triple_weight,
    merge_weight,
    expand_weight,
    shrink_weight,
    vector_params,
    triple_moment,
    merge_moment,
    expand_moment,
    shrink_moment,
    vector_moment,
    triple_square,
    merge_square,
    expand_square,
    shrink_square,
    vector_square,
):
    bf16 = jnp.bfloat16
    f32 = jnp.float32
    n = lax.axis_size("ctx")
    m = lax.axis_size("dp")
    here = lax.axis_index("ctx")
    seq_here = lax.axis_index("dp")
    chips = n // 2
    rows = inputs.shape[1]
    total = rows * n
    feat = D // n
    cut = n * TILE
    spare = D - cut
    wide = expand_weight.shape[1]
    hid = shrink_weight.shape[0]
    fold = wide // hid
    cols = shrink_weight.shape[1]
    stream = inputs[0]
    cotangent = out_grad[0]
    tw, mw = triple_weight.shape[1], merge_weight.shape[1]

    flat = pair_blocks.reshape(-1)
    blocks = jnp.arange(flat.shape[0], dtype=jnp.int32)
    order = jnp.sum(jnp.where(flat[None, :] == blocks[:, None], blocks[None, :], 0), axis=1)

    w_expand_own = expand_weight.astype(bf16)
    w_shrink_own = (
        shrink_weight.astype(bf16)
        .T.reshape(fold, cols // fold, hid)
        .transpose(1, 0, 2)
        .reshape(cols // fold, wide)
    )
    packed = jnp.concatenate(
        [triple_weight.astype(bf16), merge_weight.astype(bf16), vector_params.astype(bf16)], axis=1
    )
    normed_one, inverse_one = layer_norm(stream)
    cot_b = cotangent.astype(bf16)
    normed_full, columns, cot_full = move(
        0, ("gather_ctx", normed_one.astype(bf16)), ("gather_dp", packed), ("gather_dp", cot_b)
    )
    normed_full = normed_full.reshape(total, D)
    cot_full = cot_full.reshape(m * rows, D)

    expand_line = line_gather(w_expand_own)
    w_expand = both_cores(expand_line, trade(expand_line), 1).reshape(D, wide)
    shrink_line = swap_dp(line_gather(w_shrink_own))
    w_shrink_t = (
        both_cores(shrink_line, trade(shrink_line), 1)
        .reshape(m, fold, cols // fold, fold, hid)
        .transpose(0, 3, 2, 1, 4)
        .reshape(D, wide)
    )

    def take(start, width):
        return columns[:, :, start : start + width].transpose(1, 0, 2).reshape(feat, m * width)

    triple_rows = take(0, tw).reshape(feat, 3, D)
    merge_rows = take(tw, mw)
    vector_rows = take(tw + mw, vector_params.shape[1])
    slabs = (
        triple_rows[:, :, :cut].reshape(feat, 3, n, TILE).transpose(2, 0, 1, 3).reshape(n, feat, -1)
    )
    common = jnp.concatenate([triple_rows[:, :, cut:].reshape(feat, 3 * spare), vector_rows], axis=1)
    w_main, w_common = move(1, ("swap_ctx", slabs), ("gather_ctx", common))
    merge_line = line_gather(merge_rows)
    w_merge = both_cores(merge_line, trade(merge_line), 1).reshape(D, D)
    w_main = w_main.reshape(D, 3, TILE)
    w_common = w_common.reshape(D, -1)
    w_last = w_common[:, : 3 * spare].reshape(D, 3, spare)
    w_last = jnp.pad(w_last, ((0, 0), (0, 0), (0, TILE - spare)))
    w_triple = jnp.concatenate([w_main, w_last], axis=2).reshape(D, 6 * TILE)
    vectors = w_common[:, 3 * spare :].astype(f32)
    gain_one = vectors[:, 0]
    shift_one = vectors[:, 1]
    merge_bias = vectors[:, 4]
    gain_two = vectors[:, 5]
    shift_two = vectors[:, 6]
    shrink_bias = vectors[:, 7]
    expand_bias = lax.dynamic_slice_in_dim(vectors[:, 8:].T.reshape(-1), seq_here * wide, wide)

    def own_bias(column):
        main = lax.dynamic_slice_in_dim(vectors[:, column], here * TILE, TILE)
        last = jnp.pad(vectors[cut:, column], (0, TILE - spare))
        return jnp.concatenate([main, last])

    zeros = jnp.zeros((2 * TILE,), f32)
    bias = jnp.concatenate([own_bias(2), zeros, own_bias(3)])
    act_one = (normed_full.astype(f32) * gain_one + shift_one).astype(bf16)
    qkv = (dot_on(act_one, w_triple, 1, 0) + bias).astype(bf16)
    rows_scratch = pltpu.VMEM((total, 6 * TILE), bf16)
    half_scratch = pltpu.VMEM((total, 2 * TILE), bf16)
    attended, log_total = attend(
        pairs_forward,
        order,
        (qkv,),
        [
            jax.ShapeDtypeStruct((total, 2 * TILE), bf16),
            jax.ShapeDtypeStruct((total, TILE), f32),
        ],
        [rows_scratch, half_scratch],
        2,
    )
    (att_main,) = move(2, ("swap_ctx", attended[:, :TILE].reshape(n, rows, TILE)))
    att_last = lax.dynamic_slice(attended, (here * rows, TILE), (rows, spare))
    att_own = jnp.concatenate(
        [att_main.transpose(1, 0, 2).reshape(rows, cut), att_last], axis=1
    )
    middle = stream + dot_on(att_own, w_merge, 1, 0) + merge_bias
    normed_two, inverse_two = layer_norm(middle)
    (act_two,) = move(3, ("gather_dp", (normed_two * gain_two + shift_two).astype(bf16)))
    act_two = act_two.reshape(m * rows, D)
    pre_act = dot_on(act_two, w_expand, 1, 0) + expand_bias
    hidden_b = gelu_value(pre_act).astype(bf16)
    dpre = dot_on(cot_full, w_shrink_t, 1, 0) * gelu_slope(pre_act)
    dpre_b = dpre.astype(bf16)
    expand_bias_grad = jnp.sum(dpre, axis=0)
    dact_part = dot_on(dpre_b, w_expand, 1, 1).astype(bf16).reshape(m, rows, D)
    (dact_two,) = move(4, ("sum_dp", dact_part))
    out_part = dot_on(hidden_b, w_shrink_t, 1, 1).astype(bf16).reshape(m, rows, D)

    expand_part = dot_on(act_two, dpre_b, 0, 0).astype(bf16).reshape(chips, 2, feat, wide)
    expand_grad = line_sum(core_sum(expand_part, 1))
    shrink_part = (
        dot_on(cot_full, hidden_b, 0, 0)
        .astype(bf16)
        .reshape(m, fold, cols // fold, fold, hid)
        .transpose(0, 3, 2, 1, 4)
        .reshape(m, fold, cols // fold, wide)
    )
    shrink_own = line_sum(swap_dp(core_sum(shrink_part, 1)))
    shrink_grad = (
        shrink_own.reshape(cols // fold, fold, hid).transpose(1, 0, 2).reshape(cols, hid).T
    )

    shrink_bias_grad = jnp.sum(cotangent, axis=0)
    gain_two_grad = jnp.sum(dact_two * normed_two, axis=0)
    shift_two_grad = jnp.sum(dact_two, axis=0)
    dmiddle = cotangent + norm_back(dact_two, normed_two, inverse_two, gain_two)
    dmiddle_b = dmiddle.astype(bf16)
    merge_bias_grad = jnp.sum(dmiddle, axis=0)
    dattended = dot_on(dmiddle_b, w_merge, 1, 1).astype(bf16)
    datt_main, datt_last = move(
        5,
        ("swap_ctx", dattended[:, :cut].reshape(rows, n, TILE).transpose(1, 0, 2)),
        ("gather_ctx", jnp.pad(dattended[:, cut:], ((0, 0), (0, TILE - spare)))),
    )
    merge_part = dot_on(att_own, dmiddle_b, 0, 0).astype(bf16).reshape(chips, 2, feat, D)
    merge_rows_grad = line_sum(core_sum(merge_part, 1))
    datt = jnp.concatenate(
        [datt_main.reshape(total, TILE), datt_last.reshape(total, TILE)], axis=1
    )
    (dqkv,) = attend(
        pairs_backward,
        order,
        (qkv, attended, log_total, datt),
        [jax.ShapeDtypeStruct((total, 6 * TILE), bf16)],
        [
            rows_scratch,
            half_scratch,
            half_scratch,
            rows_scratch,
            pltpu.VMEM((2 * TILE, total), f32),
            pltpu.VMEM((2 * TILE, total), f32),
        ],
        5,
    )
    lane = lax.broadcasted_iota(jnp.int32, (1, 6 * TILE), 1)
    counted = ((lane // TILE) % 2 == 0) | (here == 0)
    w_counted = jnp.where(counted, w_triple, jnp.zeros_like(w_triple))
    dact_part = dot_on(dqkv, w_counted, 1, 1).astype(bf16).reshape(n, rows, D)
    dact_one, out_sum = move(6, ("sum_ctx", dact_part), ("sum_dp", out_part))
    block_out = middle + out_sum + shrink_bias
    bias_grads = jnp.where(counted[0], jnp.sum(dqkv.astype(f32), axis=0), 0.0)
    gain_one_grad = jnp.sum(dact_one * normed_one, axis=0)
    shift_one_grad = jnp.sum(dact_one, axis=0)
    input_rows = dmiddle + norm_back(dact_one, normed_one, inverse_one, gain_one)

    def place(part):
        main = lax.dynamic_update_slice_in_dim(
            jnp.zeros((cut,), f32), bias_grads[2 * part * TILE :][:TILE], here * TILE, 0
        )
        return jnp.concatenate([main, bias_grads[(2 * part + 1) * TILE :][:spare]])

    expand_bias_all = lax.dynamic_update_slice_in_dim(
        jnp.zeros((m * wide,), f32), expand_bias_grad, seq_here * wide, 0
    )
    vector_local = jnp.concatenate(
        [
            jnp.stack(
                [
                    gain_one_grad,
                    shift_one_grad,
                    place(0),
                    place(2),
                    merge_bias_grad,
                    gain_two_grad,
                    shift_two_grad,
                    shrink_bias_grad,
                ],
                axis=1,
            ),
            expand_bias_all.reshape(-1, D).T,
        ],
        axis=1,
    )
    triple_part = dot_on(act_one, dqkv, 0, 0).astype(bf16).reshape(D, 3, 2, TILE)
    triple_main, vector_rows_grad = move(
        7,
        ("swap_ctx", triple_part[:, :, 0].reshape(n, feat, 3 * TILE)),
        ("sum_ctx", vector_local.reshape(n, feat, -1)),
    )
    triple_last = lax.dynamic_slice_in_dim(triple_part[:, :, 1, :spare], here * feat, feat, 0)
    triple_rows_grad = jnp.concatenate(
        [
            triple_main.reshape(n, feat, 3, TILE).transpose(1, 2, 0, 3).reshape(feat, 3, cut),
            triple_last,
        ],
        axis=2,
    )

    def by_dp(rows_part):
        return rows_part.reshape(feat, m, -1).transpose(1, 0, 2).astype(bf16)

    (last,) = move(
        8,
        (
            "sum_dp",
            jnp.concatenate(
                [by_dp(triple_rows_grad), by_dp(merge_rows_grad), by_dp(vector_rows_grad)], axis=2
            ),
        ),
    )
    triple_grad = last[:, :tw]
    merge_grad = last[:, tw : tw + mw]
    vector_grad = last[:, tw + mw :]
    triple_new, triple_moment_new, triple_square_new = adam_update(
        triple_weight, triple_grad, triple_moment, triple_square, True
    )
    merge_new, merge_moment_new, merge_square_new = adam_update(
        merge_weight, merge_grad, merge_moment, merge_square, True
    )
    expand_new, expand_moment_new, expand_square_new = adam_update(
        expand_weight, expand_grad, expand_moment, expand_square, True
    )
    shrink_new, shrink_moment_new, shrink_square_new = adam_update(
        shrink_weight, shrink_grad, shrink_moment, shrink_square, True
    )
    vector_new, vector_moment_new, vector_square_new = adam_update(
        vector_params, vector_grad, vector_moment, vector_square, False
    )
    return (
        block_out[None],
        input_rows[None],
        triple_grad,
        merge_grad,
        expand_grad,
        shrink_grad,
        vector_grad,
        triple_new,
        merge_new,
        expand_new,
        shrink_new,
        vector_new,
        triple_moment_new,
        merge_moment_new,
        expand_moment_new,
        shrink_moment_new,
        vector_moment_new,
        triple_square_new,
        merge_square_new,
        expand_square_new,
        shrink_square_new,
        vector_square_new,
    )


def solution(mesh):
    heads = H // 2
    even = mesh.shape["ctx"] == heads == 2 * mesh.shape["dp"]
    local = local_pairs if even else local_wide
    in_specs = (
        P("dp", "ctx", None),
        P("dp", "ctx", None),
        P(),
        P("ctx", "dp"),
        P("ctx", "dp"),
        P("ctx", "dp"),
        P("ctx", "dp"),
        P("ctx", "dp"),
        P("ctx", "dp"),
        P("ctx", "dp"),
        P("ctx", "dp"),
        P("ctx", "dp"),
        P("ctx", "dp"),
        P("ctx", "dp"),
        P("ctx", "dp"),
        P("ctx", "dp"),
        P("ctx", "dp"),
        P("ctx", "dp"),
    )
    out_specs = (
        P("dp", "ctx", None),
        P("dp", "ctx", None),
        P("ctx", "dp"),
        P("ctx", "dp"),
        P("ctx", "dp"),
        P("ctx", "dp"),
        P("ctx", "dp"),
        P("ctx", "dp"),
        P("ctx", "dp"),
        P("ctx", "dp"),
        P("ctx", "dp"),
        P("ctx", "dp"),
        P("ctx", "dp"),
        P("ctx", "dp"),
        P("ctx", "dp"),
        P("ctx", "dp"),
        P("ctx", "dp"),
        P("ctx", "dp"),
        P("ctx", "dp"),
        P("ctx", "dp"),
        P("ctx", "dp"),
        P("ctx", "dp"),
    )
    return jax.shard_map(local, mesh=mesh, in_specs=in_specs, out_specs=out_specs, check_vma=False)
```

```python
import jax
import jax.numpy as jnp
from jax import lax
from jax.experimental import pallas as pl
from jax.experimental.pallas import tpu as pltpu
from jax.sharding import PartitionSpec as P

D = 1088
H = 17
HD = 64
BLK = 64


norm_eps = 1e-05
beta_first = 0.9
beta_second = 0.95
learn_rate = 0.01
decay_rate = 0.1
adam_eps = 1e-08
adam_steps = 4
gelu_coef = 0.7978845608028654
masked_score = -1e30


def layer_norm(values):
    center = jnp.mean(values, axis=-1, keepdims=True)
    shifted = values - center
    inverse = lax.rsqrt(jnp.mean(shifted * shifted, axis=-1, keepdims=True) + norm_eps)
    return (shifted * inverse, inverse)


def norm_back(incoming, normed, inverse, gain_vec):
    scaled = incoming * gain_vec
    return inverse * (
        scaled
        - jnp.mean(scaled, axis=-1, keepdims=True)
        - normed * jnp.mean(scaled * normed, axis=-1, keepdims=True)
    )


def gelu_value(values):
    inside = gelu_coef * (values + 0.044715 * values * values * values)
    return 0.5 * values * (1.0 + jnp.tanh(inside))


def gelu_slope(values):
    inside = gelu_coef * (values + 0.044715 * values * values * values)
    tangent = jnp.tanh(inside)
    return 0.5 * (1.0 + tangent) + 0.5 * values * (1.0 - tangent * tangent) * gelu_coef * (
        1.0 + 3.0 * 0.044715 * values * values
    )


def adam_update(weight, gradient, moment, square, decayed):
    moment_new = beta_first * moment + (1.0 - beta_first) * gradient
    square_new = beta_second * square + (1.0 - beta_second) * gradient * gradient
    first_fix = 1.0 - beta_first**adam_steps
    second_fix = 1.0 - beta_second**adam_steps
    direction = moment_new / first_fix / (jnp.sqrt(square_new / second_fix) + adam_eps)
    if decayed:
        direction = direction + decay_rate * weight
    return (weight - learn_rate * direction, moment_new, square_new)


def dot_on(left, right, left_dim, right_dim):
    return lax.dot_general(
        left, right, (((left_dim,), (right_dim,)), ((), ())), preferred_element_type=jnp.float32
    )


def head_probs(query_t, key_t, allowed):
    scores = dot_on(query_t, key_t, 0, 0) * HD ** (-0.5)
    scores = jnp.where(allowed, scores, masked_score)
    row_max = jnp.max(scores, axis=1, keepdims=True)
    weights = jnp.exp(scores - row_max)
    return weights / jnp.sum(weights, axis=1, keepdims=True)


def forward_kernel(query_pos, key_pos, query_ref, key_ref, value_ref, out_ref):
    allowed = query_pos[...] >= key_pos[...]
    probs = head_probs(query_ref[...], key_ref[...], allowed).astype(jnp.bfloat16)
    out_ref[...] = dot_on(value_ref[...], probs, 1, 1).astype(jnp.bfloat16)


def backward_kernel(
    query_pos, key_pos, query_ref, key_ref, value_ref, out_ref, dout_ref, dquery, dkey, dvalue
):
    allowed = query_pos[...] >= key_pos[...]
    query_t = query_ref[...]
    key_t = key_ref[...]
    dout_t = dout_ref[...]
    probs = head_probs(query_t, key_t, allowed)
    dprobs = dot_on(dout_t, value_ref[...], 0, 0)
    products = dout_t.astype(jnp.float32) * out_ref[...].astype(jnp.float32)
    delta = jnp.sum(products.T, axis=1, keepdims=True)
    dscores = (probs * (dprobs - delta) * HD ** (-0.5)).astype(jnp.bfloat16)
    dquery[...] = dot_on(key_t, dscores, 1, 1).astype(jnp.bfloat16)
    dkey[...] = dot_on(query_t, dscores, 1, 0).astype(jnp.bfloat16)
    dvalue[...] = dot_on(dout_t, probs.astype(jnp.bfloat16), 1, 0).astype(jnp.bfloat16)


def attention(kernel, query_pos, key_pos, features, out_rows):
    queries, keys = query_pos.shape[0], key_pos.shape[1]
    whole = lambda array: pl.BlockSpec(array.shape, lambda h: (0, 0))
    block = lambda width: pl.BlockSpec((HD, width), lambda h: (h, 0))
    shapes = [jax.ShapeDtypeStruct((H * HD, width), jnp.bfloat16) for width in out_rows]
    flops = 2 * H * HD * queries * keys * (2 if len(out_rows) == 1 else 5)
    return pl.pallas_call(
        kernel,
        grid=(H,),
        in_specs=[whole(query_pos), whole(key_pos)] + [block(x.shape[1]) for x in features],
        out_specs=[block(width) for width in out_rows],
        out_shape=shapes,
        cost_estimate=pl.CostEstimate(
            flops=flops, bytes_accessed=8 * H * HD * keys, transcendentals=H * queries * keys
        ),
    )(query_pos, key_pos, *features)


def exchange(blocks):
    return lax.all_to_all(blocks, "ctx", split_axis=0, concat_axis=0, tiled=True)


def scatter_rows(partial):
    return lax.psum_scatter(
        partial.astype(jnp.bfloat16), "ctx", scatter_dimension=0, tiled=True
    ).astype(jnp.float32)


def gather_rows(rows):
    return lax.all_gather(rows, "ctx", axis=0, tiled=True)


def local_wide(
    inputs,
    out_grad,
    pair_blocks,
    triple_weight,
    merge_weight,
    expand_weight,
    shrink_weight,
    vector_params,
    triple_moment,
    merge_moment,
    expand_moment,
    shrink_moment,
    vector_moment,
    triple_square,
    merge_square,
    expand_square,
    shrink_square,
    vector_square,
):
    bf16 = jnp.bfloat16
    n = lax.axis_size("ctx")
    m = lax.axis_size("dp")
    here = lax.axis_index("ctx")
    rows = inputs.shape[1]
    total = rows * n
    feat = D // n
    hidden_width = m * expand_weight.shape[1]
    wide = hidden_width // n
    stream = inputs[0]
    cotangent = out_grad[0]
    offsets = jnp.arange(BLK, dtype=jnp.int32)
    positions = (pair_blocks.reshape(-1)[:, None] * BLK + offsets[None, :]).reshape(-1)
    query_pos = lax.dynamic_slice_in_dim(positions, here * rows, rows)[:, None]
    key_pos = positions[None, :]

    packed = jnp.concatenate(
        [
            triple_weight.astype(bf16),
            merge_weight.astype(bf16),
            expand_weight.astype(bf16),
            vector_params.astype(bf16),
        ],
        axis=1,
    )
    tw, mw, ew = triple_weight.shape[1], merge_weight.shape[1], expand_weight.shape[1]
    columns = lax.all_gather(packed, "dp", axis=0)

    def take(start, width):
        return columns[:, :, start : start + width].transpose(1, 0, 2).reshape(feat, m * width)

    triple_rows = take(0, tw)
    merge_rows = take(tw, mw)
    expand_rows = take(tw + mw, ew)
    vector_rows = take(tw + mw + ew, vector_params.shape[1])
    normed_one, inverse_one = layer_norm(stream)
    normed_full = gather_rows(normed_one.astype(bf16))
    send = jnp.concatenate(
        [
            triple_rows.reshape(feat, 3, n, feat).transpose(2, 0, 1, 3).reshape(n, feat, 3 * feat),
            expand_rows.reshape(feat, n, wide).transpose(1, 0, 2),
        ],
        axis=2,
    )
    got = exchange(send).reshape(D, 3 * feat + wide)
    w_triple = got[:, : 3 * feat]
    w_expand = got[:, 3 * feat :]
    merged = gather_rows(jnp.concatenate([merge_rows, vector_rows], axis=1))
    w_merge = merged[:, :D]
    vectors = merged[:, D:].astype(jnp.float32)
    gain_one = vectors[:, 0]
    shift_one = vectors[:, 1]
    query_bias = lax.dynamic_slice_in_dim(vectors[:, 2], here * feat, feat)
    value_bias = lax.dynamic_slice_in_dim(vectors[:, 3], here * feat, feat)
    merge_bias = vectors[:, 4]
    gain_two = vectors[:, 5]
    shift_two = vectors[:, 6]
    shrink_bias = vectors[:, 7]
    expand_bias = lax.dynamic_slice_in_dim(vectors[:, 8:].T.reshape(-1), here * wide, wide)

    act_one = (normed_full.astype(jnp.float32) * gain_one + shift_one).astype(bf16)
    bias = jnp.concatenate([query_bias, jnp.zeros_like(query_bias), value_bias])
    triple_t = (dot_on(w_triple, act_one, 0, 1) + bias[:, None]).astype(bf16)
    query_t = exchange(triple_t[:feat].reshape(feat, n, rows).transpose(1, 0, 2)).reshape(D, rows)
    both = lax.all_gather(triple_t[feat:].reshape(2, feat, total), "ctx", axis=0)
    key_t = both[:, 0].reshape(D, total)
    value_t = both[:, 1].reshape(D, total)
    (attended_t,) = attention(
        forward_kernel, query_pos, key_pos, (query_t, key_t, value_t), (rows,)
    )
    cot_full = gather_rows(cotangent.astype(bf16))
    w_shrink = (
        lax.all_gather(shrink_weight.astype(bf16), "dp", axis=0).transpose(1, 0, 2).reshape(wide, D)
    )
    middle = stream + dot_on(attended_t, w_merge, 0, 0) + merge_bias
    normed_two, inverse_two = layer_norm(middle)
    act_two = gather_rows((normed_two * gain_two + shift_two).astype(bf16))
    pre_act = dot_on(act_two, w_expand, 1, 0) + expand_bias
    hidden_b = gelu_value(pre_act).astype(bf16)
    dpre = dot_on(cot_full, w_shrink, 1, 1) * gelu_slope(pre_act)
    dpre_b = dpre.astype(bf16)
    expand_bias_grad = jnp.sum(dpre, axis=0)
    dact_two = scatter_rows(dot_on(dpre_b, w_expand, 1, 1))
    block_out = middle + scatter_rows(dot_on(hidden_b, w_shrink, 1, 0)) + shrink_bias
    shrink_part = dot_on(hidden_b, cot_full, 0, 0).astype(bf16)
    expand_part = dot_on(act_two, dpre_b, 0, 0).astype(bf16)
    shrink_grad = lax.psum_scatter(
        shrink_part.reshape(wide, m, D // m).transpose(1, 0, 2), "dp", scatter_dimension=0
    ).astype(jnp.float32)
    shrink_bias_grad = jnp.sum(cotangent, axis=0)
    gain_two_grad = jnp.sum(dact_two * normed_two, axis=0)
    shift_two_grad = jnp.sum(dact_two, axis=0)
    dmiddle = cotangent + norm_back(dact_two, normed_two, inverse_two, gain_two)
    dmiddle_b = dmiddle.astype(bf16)
    merge_part = lax.psum_scatter(
        dot_on(attended_t, dmiddle_b, 1, 0).astype(bf16), "ctx", scatter_dimension=0, tiled=True
    )
    merge_bias_grad = jnp.sum(dmiddle, axis=0)
    dattended_t = dot_on(w_merge, dmiddle_b, 1, 1).astype(bf16)
    dquery_t, dkey_t, dvalue_t = attention(
        backward_kernel,
        query_pos,
        key_pos,
        (query_t, key_t, value_t, attended_t, dattended_t),
        (rows, total, total),
    )
    dquery_c = exchange(dquery_t.reshape(n, feat, rows)).transpose(1, 0, 2).reshape(feat, total)
    dkey_c = lax.psum_scatter(dkey_t, "ctx", scatter_dimension=0, tiled=True)
    dvalue_c = lax.psum_scatter(dvalue_t, "ctx", scatter_dimension=0, tiled=True)
    dtriple_t = jnp.concatenate([dquery_c, dkey_c, dvalue_c], axis=0)
    query_bias_grad = jnp.sum(dquery_c.astype(jnp.float32), axis=1)
    value_bias_grad = jnp.sum(dvalue_c.astype(jnp.float32), axis=1)
    dact_one = scatter_rows(dot_on(dtriple_t, w_triple, 0, 1))
    triple_part = dot_on(act_one, dtriple_t, 0, 1).astype(bf16)
    gain_one_grad = jnp.sum(dact_one * normed_one, axis=0)
    shift_one_grad = jnp.sum(dact_one, axis=0)
    input_rows = dmiddle + norm_back(dact_one, normed_one, inverse_one, gain_one)

    def place(piece, size):
        return lax.dynamic_update_slice_in_dim(
            jnp.zeros((size,), jnp.float32), piece, here * piece.shape[0], 0
        )

    vector_local = jnp.concatenate(
        [
            jnp.stack(
                [
                    gain_one_grad,
                    shift_one_grad,
                    place(query_bias_grad, D),
                    place(value_bias_grad, D),
                    merge_bias_grad,
                    gain_two_grad,
                    shift_two_grad,
                    shrink_bias_grad,
                ],
                axis=1,
            ),
            place(expand_bias_grad, hidden_width).reshape(-1, D).T,
        ],
        axis=1,
    )
    vector_part = lax.psum_scatter(vector_local, "ctx", scatter_dimension=0, tiled=True)

    def by_dp(rows_part):
        return rows_part.reshape(feat, m, -1).transpose(1, 0, 2)

    expand_rows_part = exchange(expand_part.reshape(n, feat, wide)).transpose(1, 0, 2)
    expand_grad = lax.psum_scatter(by_dp(expand_rows_part), "dp", scatter_dimension=0).astype(
        jnp.float32
    )
    triple_rows_part = (
        exchange(triple_part.reshape(n, feat, 3 * feat))
        .reshape(n, feat, 3, feat)
        .transpose(1, 2, 0, 3)
    )
    last = lax.psum_scatter(
        jnp.concatenate(
            [by_dp(triple_rows_part), by_dp(merge_part), by_dp(vector_part).astype(bf16)], axis=2
        ),
        "dp",
        scatter_dimension=0,
    ).astype(jnp.float32)
    triple_grad = last[:, :tw]
    merge_grad = last[:, tw : tw + mw]
    vector_grad = last[:, tw + mw :]
    triple_new, triple_moment_new, triple_square_new = adam_update(
        triple_weight, triple_grad, triple_moment, triple_square, True
    )
    merge_new, merge_moment_new, merge_square_new = adam_update(
        merge_weight, merge_grad, merge_moment, merge_square, True
    )
    expand_new, expand_moment_new, expand_square_new = adam_update(
        expand_weight, expand_grad, expand_moment, expand_square, True
    )
    shrink_new, shrink_moment_new, shrink_square_new = adam_update(
        shrink_weight, shrink_grad, shrink_moment, shrink_square, True
    )
    vector_new, vector_moment_new, vector_square_new = adam_update(
        vector_params, vector_grad, vector_moment, vector_square, False
    )
    return (
        block_out[None],
        input_rows[None],
        triple_grad,
        merge_grad,
        expand_grad,
        shrink_grad,
        vector_grad,
        triple_new,
        merge_new,
        expand_new,
        shrink_new,
        vector_new,
        triple_moment_new,
        merge_moment_new,
        expand_moment_new,
        shrink_moment_new,
        vector_moment_new,
        triple_square_new,
        merge_square_new,
        expand_square_new,
        shrink_square_new,
        vector_square_new,
    )


TILE = 2 * HD


def peers_of(kinds):
    me_c = lax.axis_index("ctx")
    me_d = lax.axis_index("dp")
    n = lax.axis_size("ctx")
    m = lax.axis_size("dp")
    chips = n // 2
    chip = lax.div(me_c, 2)
    core = lax.rem(me_c, 2)
    found = []
    if any("dp" in kind for kind in kinds):
        found += [{"dp": lax.rem(me_d + r, m)} for r in range(1, m)]
    if "swap_ctx" in kinds:
        found += [{"ctx": lax.rem(me_c + r, n)} for r in range(1, n)]
    elif any(kind.endswith("ctx") for kind in kinds):
        found += [{"ctx": 2 * lax.rem(chip + r, chips) + core} for r in range(1, chips)]
        found += [{"ctx": 2 * chip + 1 - core}]
    return found


def send(src, dst, send_sem, recv_sem, device):
    return pltpu.make_async_remote_copy(
        src_ref=src,
        dst_ref=dst,
        send_sem=send_sem,
        recv_sem=recv_sem,
        device_id=device,
        device_id_type=pl.DeviceIdType.MESH,
    )


class GatherDp:
    scratch = 0

    def __init__(self, x, out, sems):
        self.x, self.out, self.sems = x, out, sems
        self.m = lax.axis_size("dp")
        self.me = lax.axis_index("dp")

    def piece(self, to):
        return self.x

    def target(self, of):
        return self.out.at[of]

    def copy(self, r, of, to):
        return send(
            self.piece(to),
            self.target(of),
            self.sems[0].at[r],
            self.sems[1].at[of],
            {"dp": to},
        )

    def start(self):
        self.sent = []
        for r in range(1, self.m):
            copy = self.copy(r, self.me, lax.rem(self.me + r, self.m))
            copy.start()
            self.sent.append(copy)
        self.keep()

    def keep(self):
        self.out[self.me] = self.x[...]

    def middle(self, t):
        pass

    def finish(self):
        for r in range(1, self.m):
            of = lax.rem(self.me + self.m - r, self.m)
            self.copy(r, of, of).wait_recv()
        for copy in self.sent:
            copy.wait_send()


class SwapDp(GatherDp):
    def piece(self, to):
        return self.x.at[to]

    def keep(self):
        self.out[self.me] = self.x[self.me]


class SumDp(SwapDp):
    scratch = 1

    def __init__(self, x, out, sems, got):
        super().__init__(x, out, sems)
        self.got = got

    def target(self, of):
        return self.got.at[of]

    def keep(self):
        pass

    def finish(self):
        super().finish()
        total = self.x[self.me].astype(jnp.float32)
        for r in range(1, self.m):
            total = total + self.got[lax.rem(self.me + r, self.m)].astype(jnp.float32)
        self.out[...] = total


class SwapCtx(SwapDp):
    def __init__(self, x, out, sems):
        self.x, self.out, self.sems = x, out, sems
        self.m = lax.axis_size("ctx")
        self.me = lax.axis_index("ctx")

    def copy(self, r, of, to):
        return send(
            self.piece(to),
            self.target(of),
            self.sems[0].at[r],
            self.sems[1].at[of],
            {"ctx": to},
        )


class Line:
    def setup(self):
        self.chips = lax.axis_size("ctx") // 2
        self.me = lax.axis_index("ctx")
        self.chip = lax.div(self.me, 2)
        self.core = lax.rem(self.me, 2)
        self.partner = 2 * self.chip + 1 - self.core
        self.sent = []

    def launch(self, copy, when=None):
        self.sent.append((copy, when))
        if when is None:
            copy.start()
        else:
            pl.when(when)(copy.start)

    def drain(self):
        for copy, when in self.sent:
            if when is None:
                copy.wait_send()
            else:
                pl.when(when)(copy.wait_send)

    def sides(self):
        return (
            (1, self.chip < self.chips - 1, self.chip > 0),
            (-1, self.chip > 0, self.chip < self.chips - 1),
        )

    def safe(self, chip):
        return lax.min(lax.max(chip, 0), self.chips - 1)


class GatherCtx(Line):
    scratch = 0

    def __init__(self, x, out, sems):
        self.x, self.out, self.sems = x, out, sems
        self.setup()

    def of_chip(self, r, core):
        return 2 * lax.rem(self.chip + self.chips + r, self.chips) + core

    def copy(self, src, slot, of, to):
        return send(
            src, self.out.at[of], self.sems[0].at[slot], self.sems[1].at[of], {"ctx": to}
        )

    def start(self):
        for side, onward, _ in self.sides():
            to = 2 * self.safe(self.chip + side) + self.core
            self.launch(self.copy(self.x, (side + 1) // 2, self.me, to), onward)
        self.launch(self.copy(self.x, 2, self.me, self.partner))
        self.out[self.me] = self.x[...]

    def middle(self, t):
        for side, onward, _ in self.sides():
            chip = self.chip - side * t
            here = (chip >= 0) & (chip < self.chips)
            of = 2 * self.safe(chip) + self.core
            slot = 3 + 4 * (t - 1) + (side + 1)
            pl.when(here)(self.copy(self.x, slot, of, of).wait_recv)
            to = 2 * self.safe(self.chip + side) + self.core
            self.launch(self.copy(self.out.at[of], slot, of, to), here & onward)
            self.launch(self.copy(self.out.at[of], slot + 1, of, self.partner), here)

    def finish(self):
        for r in range(self.chips):
            of = self.of_chip(-r, 1 - self.core)
            self.copy(self.x, 2, of, self.partner).wait_recv()
        self.drain()


class ShrinkGather(Line):
    scratch = 1

    def __init__(self, x, out, sems, line):
        self.x, self.out, self.sems, self.line = x, out, sems, line
        self.setup()
        self.m = lax.axis_size("dp")
        self.row = lax.axis_index("dp")

    def along(self, src, slot, of, to):
        return send(
            src, self.line.at[of], self.sems[0].at[slot], self.sems[1].at[of],
            {"ctx": 2 * to + self.core},
        )

    def across(self, src, slot, of, to):
        return send(
            src, self.out.at[of, self.core], self.sems[0].at[slot],
            self.sems[1].at[self.chips + of], {"dp": to},
        )

    def over(self, slot, of, core):
        return send(
            self.out.at[of, core], self.out.at[of, core], self.sems[0].at[slot],
            self.sems[1].at[self.chips + self.m + of], {"ctx": self.partner},
        )

    def place(self, src, chip, slot, when):
        mine = chip == self.row
        ok = mine if when is None else when & mine

        @pl.when(ok)
        def _():
            self.out[self.row, self.core] = src[...]

        other = chip != self.row
        to = lax.rem(chip + 0 * self.row, self.m)
        self.launch(self.across(src, slot, self.row, to), other if when is None else when & other)

    def start(self):
        for side, onward, _ in self.sides():
            to = self.safe(self.chip + side)
            self.launch(self.along(self.x, (side + 1) // 2, self.chip, to), onward)
        self.place(self.x, self.chip, 2, None)

    def middle(self, t):
        for side, onward, _ in self.sides():
            chip = self.chip - side * t
            here = (chip >= 0) & (chip < self.chips)
            of = self.safe(chip)
            slot = 3 + 4 * (t - 1) + (side + 1)
            pl.when(here)(self.along(self.x, slot, of, of).wait_recv)
            to = self.safe(self.chip + side)
            self.launch(self.along(self.line.at[of], slot, of, to), here & onward)
            self.place(self.line.at[of], of, slot + 1, here)

    def finish(self):
        base = 3 + 4 * (self.chips - 1)
        self.launch(self.over(base, self.row, self.core))
        for r in range(1, self.m):
            of = lax.rem(self.row + r, self.m)
            self.across(self.x, 2, of, of).wait_recv()
            self.launch(self.over(base + r, of, self.core))
        for of in range(self.m):
            self.over(base, of, 1 - self.core).wait_recv()
        self.drain()


class SumCtx(Line):
    scratch = 3

    def __init__(self, x, out, sems, half, pre, got):
        self.x, self.out, self.sems = x, out, sems
        self.half, self.pre, self.got = half, pre, got
        self.setup()

    def early(self, r):
        j = lax.rem(self.chip + r, self.chips)
        return send(
            self.x.at[2 * j + 1 - self.core],
            self.half.at[j],
            self.sems[0].at[r],
            self.sems[1].at[j],
            {"ctx": self.partner},
        )

    def late(self, r, of, to):
        return send(
            self.pre.at[to],
            self.got.at[of],
            self.sems[0].at[self.chips + r],
            self.sems[1].at[self.chips + of],
            {"ctx": 2 * to + self.core},
        )

    def start(self):
        for r in list(range(1, self.chips)) + [0]:
            self.launch(self.early(r))

    def middle(self, r):
        self.early(r).wait_recv()
        to = lax.rem(self.chip + r, self.chips)
        total = self.x[2 * to + self.core].astype(jnp.float32) + self.half[to].astype(jnp.float32)
        self.pre[to] = total.astype(self.pre.dtype)
        self.launch(self.late(r, self.chip, to))

    def finish(self):
        self.early(0).wait_recv()
        total = self.x[self.me].astype(jnp.float32) + self.half[self.chip].astype(jnp.float32)
        for r in range(1, self.chips):
            of = lax.rem(self.chip + self.chips - r, self.chips)
            self.late(r, of, of).wait_recv()
            total = total + self.got[of].astype(jnp.float32)
        self.out[...] = total
        self.drain()


class ShrinkCross(Line):
    scratch = 2

    def __init__(self, x, out, sems, half, pre):
        self.x, self.out, self.sems = x, out, sems
        self.half, self.pre = half, pre
        self.setup()
        self.m = lax.axis_size("dp")
        self.row = lax.axis_index("dp")

    def early(self, r):
        j = lax.rem(self.row + r, self.m)
        return send(
            self.x.at[j, 1 - self.core],
            self.half.at[j],
            self.sems[0].at[r],
            self.sems[1].at[j],
            {"ctx": self.partner},
        )

    def across(self, r, of, to):
        return send(
            self.pre.at[to],
            self.out.at[of],
            self.sems[0].at[self.m + r],
            self.sems[1].at[self.m + of],
            {"dp": to},
        )

    def add(self, j):
        total = self.x[j, self.core].astype(jnp.float32) + self.half[j].astype(jnp.float32)
        return total.astype(self.pre.dtype)

    def start(self):
        for r in list(range(1, self.m)) + [0]:
            self.launch(self.early(r))

    def middle(self, r):
        self.early(r).wait_recv()
        to = lax.rem(self.row + r, self.m)
        self.pre[to] = self.add(to)
        self.launch(self.across(r, self.row, to))

    def finish(self):
        self.early(0).wait_recv()
        self.out[self.row] = self.add(self.row)
        for r in range(1, self.m):
            of = lax.rem(self.row + self.m - r, self.m)
            self.across(r, of, of).wait_recv()
        self.drain()


class LineSum(Line):
    scratch = 1

    def __init__(self, x, out, sems, got):
        self.x, self.out, self.sems, self.got = x, out, sems, got
        self.setup()

    def along(self, r, of, to):
        return send(
            self.x.at[to],
            self.got.at[of],
            self.sems[0].at[r],
            self.sems[1].at[of],
            {"ctx": 2 * to + self.core},
        )

    def start(self):
        for r in range(1, self.chips):
            self.launch(self.along(r, self.chip, lax.rem(self.chip + r, self.chips)))

    def middle(self, t):
        pass

    def finish(self):
        total = self.x[self.chip].astype(jnp.float32)
        for r in range(1, self.chips):
            of = lax.rem(self.chip + self.chips - r, self.chips)
            self.along(r, of, of).wait_recv()
            total = total + self.got[of].astype(jnp.float32)
        self.out[...] = total
        self.drain()


class HalfGather(Line):
    scratch = 0

    def __init__(self, x, out, sems):
        self.x, self.out, self.sems = x, out, sems
        self.setup()
        self.m = lax.axis_size("dp")
        self.row = lax.axis_index("dp")

    def across(self, r, of, to):
        return send(
            self.x.at[self.core],
            self.out.at[of, self.core],
            self.sems[0].at[r],
            self.sems[1].at[of],
            {"dp": to},
        )

    def over(self, r, of, core):
        return send(
            self.out.at[of, core],
            self.out.at[of, core],
            self.sems[0].at[self.m + r],
            self.sems[1].at[self.m + of],
            {"ctx": self.partner},
        )

    def start(self):
        for r in range(1, self.m):
            self.launch(self.across(r, self.row, lax.rem(self.row + r, self.m)))
        self.out[self.row] = self.x[...]

    def middle(self, r):
        of = lax.rem(self.row + self.m - r, self.m)
        self.across(r, of, of).wait_recv()
        self.launch(self.over(r, of, self.core))

    def finish(self):
        for r in range(1, self.m):
            self.over(r, lax.rem(self.row + r, self.m), 1 - self.core).wait_recv()
        self.drain()


MOVES = {
    "gather_dp": GatherDp,
    "swap_dp": SwapDp,
    "sum_dp": SumDp,
    "gather_ctx": GatherCtx,
    "swap_ctx": SwapCtx,
    "sum_ctx": SumCtx,
    "shrink_gather_dp_ctx": ShrinkGather,
    "shrink_cross_dp_ctx": ShrinkCross,
    "line_sum_ctx": LineSum,
    "half_gather_dp_ctx": HalfGather,
}


def move_kernel(kinds, *refs):
    count = len(kinds)
    xs, outs, rest = refs[:count], refs[count : 2 * count], list(refs[2 * count :])
    barrier = pltpu.get_barrier_semaphore()
    peers = peers_of(kinds)
    for peer in peers:
        pl.semaphore_signal(
            barrier, inc=1, device_id=peer, device_id_type=pl.DeviceIdType.MESH
        )
    pl.semaphore_wait(barrier, len(peers))
    moves = []
    for kind, x, out in zip(kinds, xs, outs):
        sems = (rest.pop(0), rest.pop(0))
        extra = [rest.pop(0) for _ in range(MOVES[kind].scratch)]
        moves.append(MOVES[kind](x, out, sems, *extra))
    for move in moves:
        move.start()
    for t in range(1, lax.axis_size("ctx") // 2):
        for move in moves:
            move.middle(t)
    for move in moves:
        move.finish()


def move(collective_id, *pairs):
    kinds = tuple(kind for kind, _ in pairs)
    n = lax.axis_size("ctx")
    m = lax.axis_size("dp")
    shapes, scratch, sent = [], [], 0
    for kind, x in pairs:
        size = n if kind.endswith("ctx") else m
        one = x.dtype
        semaphores = size
        sent += x.size * x.dtype.itemsize
        extra = []
        if kind == "shrink_gather_dp_ctx":
            shape = jax.ShapeDtypeStruct((m, 2) + x.shape, one)
            extra = [pltpu.VMEM((n // 2,) + x.shape, one)]
            semaphores = 2 * n + m
        elif kind == "shrink_cross_dp_ctx":
            shape = jax.ShapeDtypeStruct((m,) + x.shape[2:], one)
            extra = [pltpu.VMEM((m,) + x.shape[2:], one)] * 2
            semaphores = 2 * m
        elif kind == "line_sum_ctx":
            shape = jax.ShapeDtypeStruct(x.shape[1:], jnp.float32)
            extra = [pltpu.VMEM(x.shape, one)]
        elif kind == "half_gather_dp_ctx":
            shape = jax.ShapeDtypeStruct((m,) + x.shape, one)
            semaphores = 2 * m
        elif kind.startswith("gather"):
            shape = jax.ShapeDtypeStruct((size,) + x.shape, one)
            semaphores = 2 * size
        elif kind.startswith("swap"):
            shape = jax.ShapeDtypeStruct(x.shape, one)
        else:
            shape = jax.ShapeDtypeStruct(x.shape[1:], jnp.float32)
            if kind == "sum_dp":
                extra = [pltpu.VMEM(x.shape, one)]
            else:
                extra = [pltpu.VMEM((n // 2,) + x.shape[1:], one)] * 3
        shapes.append(shape)
        scratch += [pltpu.SemaphoreType.DMA((semaphores,))] * 2 + extra
    kernel = lambda *refs: move_kernel(kinds, *refs)
    return pl.pallas_call(
        kernel,
        in_specs=[pl.BlockSpec(memory_space=pltpu.VMEM)] * len(kinds),
        out_specs=[pl.BlockSpec(memory_space=pltpu.VMEM)] * len(kinds),
        out_shape=shapes,
        scratch_shapes=scratch,
        compiler_params=pltpu.CompilerParams(
            collective_id=collective_id, has_side_effects=True
        ),
        cost_estimate=pl.CostEstimate(flops=sent * 100, bytes_accessed=sent, transcendentals=0),
        name="move_" + str(collective_id),
    )(*[x for _, x in pairs])


def pair_lanes(shape, half):
    lane = lax.broadcasted_iota(jnp.int32, shape, 1)
    return (lane < HD) if half == 0 else (lane >= HD)


def causal(shape):
    row = lax.broadcasted_iota(jnp.int32, shape, 0)
    return row >= lax.broadcasted_iota(jnp.int32, shape, 1)


def sort_rows(order_ref, src, dst, lane):
    for b in range(src.shape[0] // BLK):
        start = pl.multiple_of(order_ref[b] * BLK, BLK)
        dst[b * BLK : (b + 1) * BLK, lane : lane + src.shape[1]] = src[pl.ds(start, BLK), :]


def unsort_rows(order_ref, src, dst, lane):
    for b in range(dst.shape[0] // BLK):
        start = pl.multiple_of(order_ref[b] * BLK, BLK)
        dst[pl.ds(start, BLK), :] = src[b * BLK : (b + 1) * BLK, lane : lane + dst.shape[1]]


def head_slots():
    return ((0, 0), (0, 1), (1, 0))


def pairs_forward(order_ref, main_ref, last_ref, out_ref, log_ref, rows, outs):
    sort_rows(order_ref, main_ref, rows, 0)
    sort_rows(order_ref, last_ref, rows, 3 * TILE)
    seq = main_ref.shape[0]
    step = min(4 * BLK, seq)
    for i in range(seq // step):
        at = slice(i * step, (i + 1) * step)
        results, logs = [], []
        for block, half in head_slots():
            lanes = lambda part: slice((3 * block + part) * TILE, (3 * block + part + 1) * TILE)
            query = rows[at, lanes(0)] * HD ** (-0.5)
            query = query.astype(jnp.bfloat16)
            if block == 0:
                query = jnp.where(pair_lanes(query.shape, half), query, jnp.zeros_like(query))
            last = dot_on(query, rows[at, lanes(1)], 1, 1)
            last = jnp.where(causal(last.shape), last, masked_score)
            top = jnp.max(last, axis=1, keepdims=True)
            if i > 0:
                early = dot_on(query, rows[: i * step, lanes(1)], 1, 1)
                top = jnp.maximum(top, jnp.max(early, axis=1, keepdims=True))
            last = jnp.exp(last - top)
            total = jnp.sum(last, axis=1, keepdims=True)
            if i > 0:
                early = jnp.exp(early - top)
                total = total + jnp.sum(early, axis=1, keepdims=True)
            scale = 1.0 / total
            result = dot_on((last * scale).astype(jnp.bfloat16), rows[at, lanes(2)], 1, 0)
            if i > 0:
                result = result + dot_on(
                    (early * scale).astype(jnp.bfloat16), rows[: i * step, lanes(2)], 1, 0
                )
            results.append(result)
            logs.append(top + jnp.log(total))
        first = pair_lanes((step, TILE), 0)
        outs[at, :TILE] = jnp.where(first, results[0], results[1]).astype(jnp.bfloat16)
        outs[at, TILE:] = results[2].astype(jnp.bfloat16)
        lane = lax.broadcasted_iota(jnp.int32, (step, TILE), 1)
        log_ref[at, :] = jnp.where(lane == 0, logs[0], jnp.where(lane == 1, logs[1], logs[2]))
    unsort_rows(order_ref, outs, out_ref, 0)


def pairs_backward(
    order_ref,
    main_ref,
    last_ref,
    out_ref,
    log_ref,
    dout_ref,
    dmain_ref,
    dlast_ref,
    rows,
    outs,
    douts,
    grads,
    dkey,
    dvalue,
):
    sort_rows(order_ref, main_ref, rows, 0)
    sort_rows(order_ref, last_ref, rows, 3 * TILE)
    sort_rows(order_ref, out_ref, outs, 0)
    sort_rows(order_ref, dout_ref, douts, 0)
    seq = main_ref.shape[0]
    step = min(4 * BLK, seq)
    dkey[...] = jnp.zeros_like(dkey)
    dvalue[...] = jnp.zeros_like(dvalue)
    for i in range(seq // step):
        at = slice(i * step, (i + 1) * step)
        dqueries = []
        for slot, (block, half) in enumerate(head_slots()):
            lanes = lambda part: slice((3 * block + part) * TILE, (3 * block + part + 1) * TILE)
            own = slice(block * TILE, (block + 1) * TILE)
            query = (rows[at, lanes(0)] * HD ** (-0.5)).astype(jnp.bfloat16)
            dout = douts[at, own]
            if block == 0:
                mask = pair_lanes(query.shape, half)
                query = jnp.where(mask, query, jnp.zeros_like(query))
                dout = jnp.where(mask, dout, jnp.zeros_like(dout))
            delta = jnp.sum(
                dout.astype(jnp.float32) * outs[at, own].astype(jnp.float32), axis=1, keepdims=True
            )
            log_total = log_ref[at, slot : slot + 1]
            dquery = None
            for keys, diagonal in ((at, True), (slice(0, i * step), False)):
                if keys.stop == 0:
                    continue
                scores = dot_on(query, rows[keys, lanes(1)], 1, 1)
                probs = jnp.exp(scores - log_total)
                if diagonal:
                    probs = jnp.where(causal(probs.shape), probs, 0.0)
                dprobs = dot_on(dout, rows[keys, lanes(2)], 1, 1)
                dscores = (probs * (dprobs - delta)).astype(jnp.bfloat16)
                part = dot_on(dscores, rows[keys, lanes(1)], 1, 0)
                dquery = part if dquery is None else dquery + part
                dkey[own, keys] += dot_on(query, dscores, 0, 0)
                dvalue[own, keys] += dot_on(dout, probs.astype(jnp.bfloat16), 0, 0)
            dqueries.append(dquery * HD ** (-0.5))
        first = pair_lanes((step, TILE), 0)
        grads[at, :TILE] = jnp.where(first, dqueries[0], dqueries[1]).astype(jnp.bfloat16)
        third = jnp.where(first, dqueries[2], 0.0)
        grads[at, 3 * TILE : 4 * TILE] = third.astype(jnp.bfloat16)
    for block in range(2):
        own = slice(block * TILE, (block + 1) * TILE)
        grads[:, (3 * block + 1) * TILE : (3 * block + 2) * TILE] = dkey[own, :].T.astype(jnp.bfloat16)
        grads[:, (3 * block + 2) * TILE : (3 * block + 3) * TILE] = dvalue[own, :].T.astype(jnp.bfloat16)
    unsort_rows(order_ref, grads, dmain_ref, 0)
    unsort_rows(order_ref, grads, dlast_ref, 3 * TILE)


def attend(kernel, order, arrays, shapes, scratch, matmuls):
    seq = arrays[0].shape[0]
    vmem = pl.BlockSpec(memory_space=pltpu.VMEM)
    return pl.pallas_call(
        kernel,
        in_specs=[pl.BlockSpec(memory_space=pltpu.SMEM)] + [vmem] * len(arrays),
        out_specs=[vmem] * len(shapes),
        out_shape=shapes,
        scratch_shapes=scratch,
        cost_estimate=pl.CostEstimate(
            flops=3 * matmuls * seq * seq * TILE,
            bytes_accessed=seq * 24 * TILE,
            transcendentals=2 * seq * seq,
        ),
    )(order, *arrays)


def trade(x):
    return lax.ppermute(x, "ctx", [(c, c ^ 1) for c in range(lax.axis_size("ctx"))])


def core_pair(mine, other, axis):
    first = lax.axis_index("ctx") % 2 == 0
    return jnp.where(
        first, jnp.concatenate([mine, other], axis), jnp.concatenate([other, mine], axis)
    )


def local_pairs(
    inputs,
    out_grad,
    pair_blocks,
    triple_weight,
    merge_weight,
    expand_weight,
    shrink_weight,
    vector_params,
    triple_moment,
    merge_moment,
    expand_moment,
    shrink_moment,
    vector_moment,
    triple_square,
    merge_square,
    expand_square,
    shrink_square,
    vector_square,
):
    bf16 = jnp.bfloat16
    f32 = jnp.float32
    n = lax.axis_size("ctx")
    m = lax.axis_size("dp")
    here = lax.axis_index("ctx")
    seq_here = lax.axis_index("dp")
    rows = inputs.shape[1]
    total = rows * n
    feat = D // n
    cut = n * TILE
    spare = D - cut
    wide = expand_weight.shape[1]
    hid = shrink_weight.shape[0]
    fold = wide // hid
    cols = shrink_weight.shape[1]
    stream = inputs[0]
    cotangent = out_grad[0]
    tw, mw = triple_weight.shape[1], merge_weight.shape[1]

    flat = pair_blocks.reshape(-1)
    blocks = jnp.arange(flat.shape[0], dtype=jnp.int32)
    order = jnp.sum(jnp.where(flat[None, :] == blocks[:, None], blocks[None, :], 0), axis=1)

    w_expand_own = expand_weight.astype(bf16)
    first_core = here % 2 == 0
    shrink_t = shrink_weight.astype(bf16).T
    upper, lower = shrink_t[: cols // fold], shrink_t[cols // fold :]
    w_shrink_own = core_pair(
        jnp.where(first_core, upper, lower), trade(jnp.where(first_core, lower, upper)), 1
    )
    packed = jnp.concatenate(
        [triple_weight.astype(bf16), vector_params.astype(bf16)], axis=1
    )
    normed_one, inverse_one = layer_norm(stream)
    cot_b = cotangent.astype(bf16)
    normed_full, w_expand, merge_line, columns, cot_full = move(
        0,
        ("gather_ctx", normed_one.astype(bf16)),
        ("gather_ctx", w_expand_own),
        ("gather_ctx", merge_weight.astype(bf16)),
        ("gather_dp", packed),
        ("gather_dp", cot_b),
    )
    normed_full = normed_full.reshape(total, D)
    cot_full = cot_full.reshape(m * rows, D)
    w_expand = w_expand.reshape(D, wide)

    def take(start, width):
        return columns[:, :, start : start + width].transpose(1, 0, 2).reshape(feat, m * width)

    triple_rows = take(0, tw).reshape(feat, 3, D)
    vector_rows = take(tw, vector_params.shape[1])
    slabs = (
        triple_rows[:, :, :cut].reshape(feat, 3, n, TILE).transpose(2, 0, 1, 3).reshape(n, feat, -1)
    )
    common = jnp.concatenate([triple_rows[:, :, cut:].reshape(feat, 3 * spare), vector_rows], axis=1)
    w_main, w_common, w_merge, w_shrink_t = move(
        1,
        ("swap_ctx", slabs),
        ("gather_ctx", common),
        ("half_gather_dp_ctx", merge_line.reshape(2, D // 2, mw)),
        ("shrink_gather_dp_ctx", w_shrink_own),
    )
    w_shrink_t = w_shrink_t.reshape(D, wide)
    w_merge = w_merge.reshape(m, D, mw).transpose(1, 0, 2).reshape(D, D)
    w_main = w_main.reshape(D, 3 * TILE)
    w_common = w_common.reshape(D, -1)
    near = lax.broadcasted_iota(jnp.int32, (w_common.shape[1], 3 * TILE), 0)
    far = lax.broadcasted_iota(jnp.int32, (w_common.shape[1], 3 * TILE), 1)
    spread = (far % TILE < spare) & (near == far // TILE * spare + far % TILE)
    w_last = dot_on(w_common, spread.astype(bf16), 1, 0).astype(bf16)
    vectors = w_common[:, 3 * spare :].astype(f32)
    gain_one = vectors[:, 0]
    shift_one = vectors[:, 1]
    merge_bias = vectors[:, 4]
    gain_two = vectors[:, 5]
    shift_two = vectors[:, 6]
    shrink_bias = vectors[:, 7]
    expand_bias = lax.dynamic_slice_in_dim(vectors[:, 8:].T.reshape(-1), seq_here * wide, wide)

    def main_bias(column):
        return lax.dynamic_slice_in_dim(vectors[:, column], here * TILE, TILE)

    def last_bias(column):
        return jnp.pad(vectors[cut:, column], (0, TILE - spare))

    zeros = jnp.zeros((TILE,), f32)
    bias_main = jnp.concatenate([main_bias(2), zeros, main_bias(3)])
    bias_last = jnp.concatenate([last_bias(2), zeros, last_bias(3)])
    act_one = (normed_full.astype(f32) * gain_one + shift_one).astype(bf16)
    qkv_main = (dot_on(act_one, w_main, 1, 0) + bias_main).astype(bf16)
    qkv_last = (dot_on(act_one, w_last, 1, 0) + bias_last).astype(bf16)
    rows_scratch = pltpu.VMEM((total, 6 * TILE), bf16)
    half_scratch = pltpu.VMEM((total, 2 * TILE), bf16)
    attended, log_total = attend(
        pairs_forward,
        order,
        (qkv_main, qkv_last),
        [
            jax.ShapeDtypeStruct((total, 2 * TILE), bf16),
            jax.ShapeDtypeStruct((total, TILE), f32),
        ],
        [rows_scratch, half_scratch],
        2,
    )
    (att_main,) = move(2, ("swap_ctx", attended[:, :TILE].reshape(n, rows, TILE)))
    att_last = lax.dynamic_slice(attended, (here * rows, TILE), (rows, spare))
    att_own = jnp.concatenate(
        [att_main.transpose(1, 0, 2).reshape(rows, cut), att_last], axis=1
    )
    middle = stream + dot_on(att_own, w_merge, 1, 0) + merge_bias
    normed_two, inverse_two = layer_norm(middle)
    (act_two,) = move(3, ("gather_dp", (normed_two * gain_two + shift_two).astype(bf16)))
    act_two = act_two.reshape(m * rows, D)
    pre_act = dot_on(act_two, w_expand, 1, 0) + expand_bias
    hidden_b = gelu_value(pre_act).astype(bf16)
    dpre = dot_on(cot_full, w_shrink_t, 1, 0) * gelu_slope(pre_act)
    dpre_b = dpre.astype(bf16)
    expand_bias_grad = jnp.sum(dpre, axis=0)
    dact_part = dot_on(dpre_b, w_expand, 1, 1).astype(bf16).reshape(m, rows, D)
    expand_part = dot_on(act_two, dpre_b, 0, 0).astype(bf16).reshape(n, feat, wide)
    dact_two, expand_grad = move(4, ("sum_dp", dact_part), ("sum_ctx", expand_part))
    out_part = dot_on(hidden_b, w_shrink_t, 1, 1).astype(bf16).reshape(m, rows, D)

    shrink_part = (
        dot_on(cot_full, hidden_b, 0, 0).astype(bf16).reshape(m, fold, cols // fold, wide)
    )

    shrink_bias_grad = jnp.sum(cotangent, axis=0)
    gain_two_grad = jnp.sum(dact_two * normed_two, axis=0)
    shift_two_grad = jnp.sum(dact_two, axis=0)
    dmiddle = cotangent + norm_back(dact_two, normed_two, inverse_two, gain_two)
    dmiddle_b = dmiddle.astype(bf16)
    merge_bias_grad = jnp.sum(dmiddle, axis=0)
    dattended = dot_on(dmiddle_b, w_merge, 1, 1).astype(bf16)
    merge_part = dot_on(att_own, dmiddle_b, 0, 0).astype(bf16).reshape(n, feat, D)
    datt_main, datt_last, merge_rows_grad = move(
        5,
        ("swap_ctx", dattended[:, :cut].reshape(rows, n, TILE).transpose(1, 0, 2)),
        ("gather_ctx", jnp.pad(dattended[:, cut:], ((0, 0), (0, TILE - spare)))),
        ("sum_ctx", merge_part),
    )
    datt = jnp.concatenate(
        [datt_main.reshape(total, TILE), datt_last.reshape(total, TILE)], axis=1
    )
    dqkv_main, dqkv_last = attend(
        pairs_backward,
        order,
        (qkv_main, qkv_last, attended, log_total, datt),
        [jax.ShapeDtypeStruct((total, 3 * TILE), bf16)] * 2,
        [
            rows_scratch,
            half_scratch,
            half_scratch,
            rows_scratch,
            pltpu.VMEM((2 * TILE, total), f32),
            pltpu.VMEM((2 * TILE, total), f32),
        ],
        5,
    )
    counted = here == 0
    dqkv_counted = jnp.where(counted, dqkv_last, jnp.zeros_like(dqkv_last))
    dact_part = dot_on(dqkv_main, w_main, 1, 1) + dot_on(dqkv_counted, w_last, 1, 1)
    dact_part = dact_part.astype(bf16).reshape(n, rows, D)
    dact_one, shrink_cross = move(
        6, ("sum_ctx", dact_part), ("shrink_cross_dp_ctx", shrink_part)
    )
    bias_grads = jnp.concatenate(
        [jnp.sum(dqkv_main.astype(f32), axis=0), jnp.sum(dqkv_counted.astype(f32), axis=0)]
    )
    gain_one_grad = jnp.sum(dact_one * normed_one, axis=0)
    shift_one_grad = jnp.sum(dact_one, axis=0)
    input_rows = dmiddle + norm_back(dact_one, normed_one, inverse_one, gain_one)

    def place(part):
        main = lax.dynamic_update_slice_in_dim(
            jnp.zeros((cut,), f32), bias_grads[part * TILE :][:TILE], here * TILE, 0
        )
        return jnp.concatenate([main, bias_grads[(3 + part) * TILE :][:spare]])

    expand_bias_all = lax.dynamic_update_slice_in_dim(
        jnp.zeros((m * wide,), f32), expand_bias_grad, seq_here * wide, 0
    )
    vector_local = jnp.concatenate(
        [
            jnp.stack(
                [
                    gain_one_grad,
                    shift_one_grad,
                    place(0),
                    place(2),
                    merge_bias_grad,
                    gain_two_grad,
                    shift_two_grad,
                    shrink_bias_grad,
                ],
                axis=1,
            ),
            expand_bias_all.reshape(-1, D).T,
        ],
        axis=1,
    )
    triple_part = dot_on(act_one, dqkv_main, 0, 0).astype(bf16).reshape(n, feat, 3 * TILE)
    triple_last = dot_on(act_one, dqkv_last, 0, 0).astype(bf16)
    triple_main, vector_rows_grad, out_sum = move(
        7,
        ("swap_ctx", triple_part),
        ("sum_ctx", vector_local.reshape(n, feat, -1)),
        ("sum_dp", out_part),
    )
    triple_last = lax.dynamic_slice_in_dim(triple_last, here * feat, feat, 0)
    triple_last = triple_last.reshape(feat, 3, TILE)[:, :, :spare]
    triple_rows_grad = jnp.concatenate(
        [
            triple_main.reshape(n, feat, 3, TILE).transpose(1, 2, 0, 3).reshape(feat, 3, cut),
            triple_last,
        ],
        axis=2,
    )

    block_out = middle + out_sum + shrink_bias

    def by_dp(rows_part):
        return rows_part.reshape(feat, m, -1).transpose(1, 0, 2).astype(bf16)

    last, shrink_sum = move(
        8,
        (
            "sum_dp",
            jnp.concatenate(
                [by_dp(triple_rows_grad), by_dp(merge_rows_grad), by_dp(vector_rows_grad)], axis=2
            ),
        ),
        ("line_sum_ctx", shrink_cross),
    )
    left, right = shrink_sum[:, :hid], shrink_sum[:, hid:]
    shrink_grad = core_pair(
        jnp.where(first_core, left, right), trade(jnp.where(first_core, right, left)), 0
    ).T
    triple_grad = last[:, :tw]
    merge_grad = last[:, tw : tw + mw]
    vector_grad = last[:, tw + mw :]
    triple_new, triple_moment_new, triple_square_new = adam_update(
        triple_weight, triple_grad, triple_moment, triple_square, True
    )
    merge_new, merge_moment_new, merge_square_new = adam_update(
        merge_weight, merge_grad, merge_moment, merge_square, True
    )
    expand_new, expand_moment_new, expand_square_new = adam_update(
        expand_weight, expand_grad, expand_moment, expand_square, True
    )
    shrink_new, shrink_moment_new, shrink_square_new = adam_update(
        shrink_weight, shrink_grad, shrink_moment, shrink_square, True
    )
    vector_new, vector_moment_new, vector_square_new = adam_update(
        vector_params, vector_grad, vector_moment, vector_square, False
    )
    return (
        block_out[None],
        input_rows[None],
        triple_grad,
        merge_grad,
        expand_grad,
        shrink_grad,
        vector_grad,
        triple_new,
        merge_new,
        expand_new,
        shrink_new,
        vector_new,
        triple_moment_new,
        merge_moment_new,
        expand_moment_new,
        shrink_moment_new,
        vector_moment_new,
        triple_square_new,
        merge_square_new,
        expand_square_new,
        shrink_square_new,
        vector_square_new,
    )


def solution(mesh):
    heads = H // 2
    even = mesh.shape["ctx"] == heads == 2 * mesh.shape["dp"]
    local = local_pairs if even else local_wide
    in_specs = (
        P("dp", "ctx", None),
        P("dp", "ctx", None),
        P(),
        P("ctx", "dp"),
        P("ctx", "dp"),
        P("ctx", "dp"),
        P("ctx", "dp"),
        P("ctx", "dp"),
        P("ctx", "dp"),
        P("ctx", "dp"),
        P("ctx", "dp"),
        P("ctx", "dp"),
        P("ctx", "dp"),
        P("ctx", "dp"),
        P("ctx", "dp"),
        P("ctx", "dp"),
        P("ctx", "dp"),
        P("ctx", "dp"),
    )
    out_specs = (
        P("dp", "ctx", None),
        P("dp", "ctx", None),
        P("ctx", "dp"),
        P("ctx", "dp"),
        P("ctx", "dp"),
        P("ctx", "dp"),
        P("ctx", "dp"),
        P("ctx", "dp"),
        P("ctx", "dp"),
        P("ctx", "dp"),
        P("ctx", "dp"),
        P("ctx", "dp"),
        P("ctx", "dp"),
        P("ctx", "dp"),
        P("ctx", "dp"),
        P("ctx", "dp"),
        P("ctx", "dp"),
        P("ctx", "dp"),
        P("ctx", "dp"),
        P("ctx", "dp"),
        P("ctx", "dp"),
        P("ctx", "dp"),
    )
    return jax.shard_map(local, mesh=mesh, in_specs=in_specs, out_specs=out_specs, check_vma=False)
```

```python
import jax
import jax.numpy as jnp
from jax import lax
from jax.experimental import pallas as pl
from jax.experimental.pallas import tpu as pltpu
from jax.sharding import PartitionSpec as P

D = 1088
H = 17
HD = 64
BLK = 64


norm_eps = 1e-05
beta_first = 0.9
beta_second = 0.95
learn_rate = 0.01
decay_rate = 0.1
adam_eps = 1e-08
adam_steps = 4
gelu_coef = 0.7978845608028654
masked_score = -1e30


def layer_norm(values):
    center = jnp.mean(values, axis=-1, keepdims=True)
    shifted = values - center
    inverse = lax.rsqrt(jnp.mean(shifted * shifted, axis=-1, keepdims=True) + norm_eps)
    return (shifted * inverse, inverse)


def norm_back(incoming, normed, inverse, gain_vec):
    scaled = incoming * gain_vec
    return inverse * (
        scaled
        - jnp.mean(scaled, axis=-1, keepdims=True)
        - normed * jnp.mean(scaled * normed, axis=-1, keepdims=True)
    )


def gelu_value(values):
    inside = gelu_coef * (values + 0.044715 * values * values * values)
    return 0.5 * values * (1.0 + jnp.tanh(inside))


def gelu_slope(values):
    inside = gelu_coef * (values + 0.044715 * values * values * values)
    tangent = jnp.tanh(inside)
    return 0.5 * (1.0 + tangent) + 0.5 * values * (1.0 - tangent * tangent) * gelu_coef * (
        1.0 + 3.0 * 0.044715 * values * values
    )


def adam_update(weight, gradient, moment, square, decayed):
    moment_new = beta_first * moment + (1.0 - beta_first) * gradient
    square_new = beta_second * square + (1.0 - beta_second) * gradient * gradient
    first_fix = 1.0 - beta_first**adam_steps
    second_fix = 1.0 - beta_second**adam_steps
    direction = moment_new / first_fix / (jnp.sqrt(square_new / second_fix) + adam_eps)
    if decayed:
        direction = direction + decay_rate * weight
    return (weight - learn_rate * direction, moment_new, square_new)


def dot_on(left, right, left_dim, right_dim):
    return lax.dot_general(
        left, right, (((left_dim,), (right_dim,)), ((), ())), preferred_element_type=jnp.float32
    )


def head_probs(query_t, key_t, allowed):
    scores = dot_on(query_t, key_t, 0, 0) * HD ** (-0.5)
    scores = jnp.where(allowed, scores, masked_score)
    row_max = jnp.max(scores, axis=1, keepdims=True)
    weights = jnp.exp(scores - row_max)
    return weights / jnp.sum(weights, axis=1, keepdims=True)


def forward_kernel(query_pos, key_pos, query_ref, key_ref, value_ref, out_ref):
    allowed = query_pos[...] >= key_pos[...]
    probs = head_probs(query_ref[...], key_ref[...], allowed).astype(jnp.bfloat16)
    out_ref[...] = dot_on(value_ref[...], probs, 1, 1).astype(jnp.bfloat16)


def backward_kernel(
    query_pos, key_pos, query_ref, key_ref, value_ref, out_ref, dout_ref, dquery, dkey, dvalue
):
    allowed = query_pos[...] >= key_pos[...]
    query_t = query_ref[...]
    key_t = key_ref[...]
    dout_t = dout_ref[...]
    probs = head_probs(query_t, key_t, allowed)
    dprobs = dot_on(dout_t, value_ref[...], 0, 0)
    products = dout_t.astype(jnp.float32) * out_ref[...].astype(jnp.float32)
    delta = jnp.sum(products.T, axis=1, keepdims=True)
    dscores = (probs * (dprobs - delta) * HD ** (-0.5)).astype(jnp.bfloat16)
    dquery[...] = dot_on(key_t, dscores, 1, 1).astype(jnp.bfloat16)
    dkey[...] = dot_on(query_t, dscores, 1, 0).astype(jnp.bfloat16)
    dvalue[...] = dot_on(dout_t, probs.astype(jnp.bfloat16), 1, 0).astype(jnp.bfloat16)


def attention(kernel, query_pos, key_pos, features, out_rows):
    queries, keys = query_pos.shape[0], key_pos.shape[1]
    whole = lambda array: pl.BlockSpec(array.shape, lambda h: (0, 0))
    block = lambda width: pl.BlockSpec((HD, width), lambda h: (h, 0))
    shapes = [jax.ShapeDtypeStruct((H * HD, width), jnp.bfloat16) for width in out_rows]
    flops = 2 * H * HD * queries * keys * (2 if len(out_rows) == 1 else 5)
    return pl.pallas_call(
        kernel,
        grid=(H,),
        in_specs=[whole(query_pos), whole(key_pos)] + [block(x.shape[1]) for x in features],
        out_specs=[block(width) for width in out_rows],
        out_shape=shapes,
        cost_estimate=pl.CostEstimate(
            flops=flops, bytes_accessed=8 * H * HD * keys, transcendentals=H * queries * keys
        ),
    )(query_pos, key_pos, *features)


def exchange(blocks):
    return lax.all_to_all(blocks, "ctx", split_axis=0, concat_axis=0, tiled=True)


def scatter_rows(partial):
    return lax.psum_scatter(
        partial.astype(jnp.bfloat16), "ctx", scatter_dimension=0, tiled=True
    ).astype(jnp.float32)


def gather_rows(rows):
    return lax.all_gather(rows, "ctx", axis=0, tiled=True)


def local_wide(
    inputs,
    out_grad,
    pair_blocks,
    triple_weight,
    merge_weight,
    expand_weight,
    shrink_weight,
    vector_params,
    triple_moment,
    merge_moment,
    expand_moment,
    shrink_moment,
    vector_moment,
    triple_square,
    merge_square,
    expand_square,
    shrink_square,
    vector_square,
):
    bf16 = jnp.bfloat16
    n = lax.axis_size("ctx")
    m = lax.axis_size("dp")
    here = lax.axis_index("ctx")
    rows = inputs.shape[1]
    total = rows * n
    feat = D // n
    hidden_width = m * expand_weight.shape[1]
    wide = hidden_width // n
    stream = inputs[0]
    cotangent = out_grad[0]
    offsets = jnp.arange(BLK, dtype=jnp.int32)
    positions = (pair_blocks.reshape(-1)[:, None] * BLK + offsets[None, :]).reshape(-1)
    query_pos = lax.dynamic_slice_in_dim(positions, here * rows, rows)[:, None]
    key_pos = positions[None, :]

    packed = jnp.concatenate(
        [
            triple_weight.astype(bf16),
            merge_weight.astype(bf16),
            expand_weight.astype(bf16),
            vector_params.astype(bf16),
        ],
        axis=1,
    )
    tw, mw, ew = triple_weight.shape[1], merge_weight.shape[1], expand_weight.shape[1]
    columns = lax.all_gather(packed, "dp", axis=0)

    def take(start, width):
        return columns[:, :, start : start + width].transpose(1, 0, 2).reshape(feat, m * width)

    triple_rows = take(0, tw)
    merge_rows = take(tw, mw)
    expand_rows = take(tw + mw, ew)
    vector_rows = take(tw + mw + ew, vector_params.shape[1])
    normed_one, inverse_one = layer_norm(stream)
    normed_full = gather_rows(normed_one.astype(bf16))
    send = jnp.concatenate(
        [
            triple_rows.reshape(feat, 3, n, feat).transpose(2, 0, 1, 3).reshape(n, feat, 3 * feat),
            expand_rows.reshape(feat, n, wide).transpose(1, 0, 2),
        ],
        axis=2,
    )
    got = exchange(send).reshape(D, 3 * feat + wide)
    w_triple = got[:, : 3 * feat]
    w_expand = got[:, 3 * feat :]
    merged = gather_rows(jnp.concatenate([merge_rows, vector_rows], axis=1))
    w_merge = merged[:, :D]
    vectors = merged[:, D:].astype(jnp.float32)
    gain_one = vectors[:, 0]
    shift_one = vectors[:, 1]
    query_bias = lax.dynamic_slice_in_dim(vectors[:, 2], here * feat, feat)
    value_bias = lax.dynamic_slice_in_dim(vectors[:, 3], here * feat, feat)
    merge_bias = vectors[:, 4]
    gain_two = vectors[:, 5]
    shift_two = vectors[:, 6]
    shrink_bias = vectors[:, 7]
    expand_bias = lax.dynamic_slice_in_dim(vectors[:, 8:].T.reshape(-1), here * wide, wide)

    act_one = (normed_full.astype(jnp.float32) * gain_one + shift_one).astype(bf16)
    bias = jnp.concatenate([query_bias, jnp.zeros_like(query_bias), value_bias])
    triple_t = (dot_on(w_triple, act_one, 0, 1) + bias[:, None]).astype(bf16)
    query_t = exchange(triple_t[:feat].reshape(feat, n, rows).transpose(1, 0, 2)).reshape(D, rows)
    both = lax.all_gather(triple_t[feat:].reshape(2, feat, total), "ctx", axis=0)
    key_t = both[:, 0].reshape(D, total)
    value_t = both[:, 1].reshape(D, total)
    (attended_t,) = attention(
        forward_kernel, query_pos, key_pos, (query_t, key_t, value_t), (rows,)
    )
    cot_full = gather_rows(cotangent.astype(bf16))
    w_shrink = (
        lax.all_gather(shrink_weight.astype(bf16), "dp", axis=0).transpose(1, 0, 2).reshape(wide, D)
    )
    middle = stream + dot_on(attended_t, w_merge, 0, 0) + merge_bias
    normed_two, inverse_two = layer_norm(middle)
    act_two = gather_rows((normed_two * gain_two + shift_two).astype(bf16))
    pre_act = dot_on(act_two, w_expand, 1, 0) + expand_bias
    hidden_b = gelu_value(pre_act).astype(bf16)
    dpre = dot_on(cot_full, w_shrink, 1, 1) * gelu_slope(pre_act)
    dpre_b = dpre.astype(bf16)
    expand_bias_grad = jnp.sum(dpre, axis=0)
    dact_two = scatter_rows(dot_on(dpre_b, w_expand, 1, 1))
    block_out = middle + scatter_rows(dot_on(hidden_b, w_shrink, 1, 0)) + shrink_bias
    shrink_part = dot_on(hidden_b, cot_full, 0, 0).astype(bf16)
    expand_part = dot_on(act_two, dpre_b, 0, 0).astype(bf16)
    shrink_grad = lax.psum_scatter(
        shrink_part.reshape(wide, m, D // m).transpose(1, 0, 2), "dp", scatter_dimension=0
    ).astype(jnp.float32)
    shrink_bias_grad = jnp.sum(cotangent, axis=0)
    gain_two_grad = jnp.sum(dact_two * normed_two, axis=0)
    shift_two_grad = jnp.sum(dact_two, axis=0)
    dmiddle = cotangent + norm_back(dact_two, normed_two, inverse_two, gain_two)
    dmiddle_b = dmiddle.astype(bf16)
    merge_part = lax.psum_scatter(
        dot_on(attended_t, dmiddle_b, 1, 0).astype(bf16), "ctx", scatter_dimension=0, tiled=True
    )
    merge_bias_grad = jnp.sum(dmiddle, axis=0)
    dattended_t = dot_on(w_merge, dmiddle_b, 1, 1).astype(bf16)
    dquery_t, dkey_t, dvalue_t = attention(
        backward_kernel,
        query_pos,
        key_pos,
        (query_t, key_t, value_t, attended_t, dattended_t),
        (rows, total, total),
    )
    dquery_c = exchange(dquery_t.reshape(n, feat, rows)).transpose(1, 0, 2).reshape(feat, total)
    dkey_c = lax.psum_scatter(dkey_t, "ctx", scatter_dimension=0, tiled=True)
    dvalue_c = lax.psum_scatter(dvalue_t, "ctx", scatter_dimension=0, tiled=True)
    dtriple_t = jnp.concatenate([dquery_c, dkey_c, dvalue_c], axis=0)
    query_bias_grad = jnp.sum(dquery_c.astype(jnp.float32), axis=1)
    value_bias_grad = jnp.sum(dvalue_c.astype(jnp.float32), axis=1)
    dact_one = scatter_rows(dot_on(dtriple_t, w_triple, 0, 1))
    triple_part = dot_on(act_one, dtriple_t, 0, 1).astype(bf16)
    gain_one_grad = jnp.sum(dact_one * normed_one, axis=0)
    shift_one_grad = jnp.sum(dact_one, axis=0)
    input_rows = dmiddle + norm_back(dact_one, normed_one, inverse_one, gain_one)

    def place(piece, size):
        return lax.dynamic_update_slice_in_dim(
            jnp.zeros((size,), jnp.float32), piece, here * piece.shape[0], 0
        )

    vector_local = jnp.concatenate(
        [
            jnp.stack(
                [
                    gain_one_grad,
                    shift_one_grad,
                    place(query_bias_grad, D),
                    place(value_bias_grad, D),
                    merge_bias_grad,
                    gain_two_grad,
                    shift_two_grad,
                    shrink_bias_grad,
                ],
                axis=1,
            ),
            place(expand_bias_grad, hidden_width).reshape(-1, D).T,
        ],
        axis=1,
    )
    vector_part = lax.psum_scatter(vector_local, "ctx", scatter_dimension=0, tiled=True)

    def by_dp(rows_part):
        return rows_part.reshape(feat, m, -1).transpose(1, 0, 2)

    expand_rows_part = exchange(expand_part.reshape(n, feat, wide)).transpose(1, 0, 2)
    expand_grad = lax.psum_scatter(by_dp(expand_rows_part), "dp", scatter_dimension=0).astype(
        jnp.float32
    )
    triple_rows_part = (
        exchange(triple_part.reshape(n, feat, 3 * feat))
        .reshape(n, feat, 3, feat)
        .transpose(1, 2, 0, 3)
    )
    last = lax.psum_scatter(
        jnp.concatenate(
            [by_dp(triple_rows_part), by_dp(merge_part), by_dp(vector_part).astype(bf16)], axis=2
        ),
        "dp",
        scatter_dimension=0,
    ).astype(jnp.float32)
    triple_grad = last[:, :tw]
    merge_grad = last[:, tw : tw + mw]
    vector_grad = last[:, tw + mw :]
    triple_new, triple_moment_new, triple_square_new = adam_update(
        triple_weight, triple_grad, triple_moment, triple_square, True
    )
    merge_new, merge_moment_new, merge_square_new = adam_update(
        merge_weight, merge_grad, merge_moment, merge_square, True
    )
    expand_new, expand_moment_new, expand_square_new = adam_update(
        expand_weight, expand_grad, expand_moment, expand_square, True
    )
    shrink_new, shrink_moment_new, shrink_square_new = adam_update(
        shrink_weight, shrink_grad, shrink_moment, shrink_square, True
    )
    vector_new, vector_moment_new, vector_square_new = adam_update(
        vector_params, vector_grad, vector_moment, vector_square, False
    )
    return (
        block_out[None],
        input_rows[None],
        triple_grad,
        merge_grad,
        expand_grad,
        shrink_grad,
        vector_grad,
        triple_new,
        merge_new,
        expand_new,
        shrink_new,
        vector_new,
        triple_moment_new,
        merge_moment_new,
        expand_moment_new,
        shrink_moment_new,
        vector_moment_new,
        triple_square_new,
        merge_square_new,
        expand_square_new,
        shrink_square_new,
        vector_square_new,
    )


TILE = 2 * HD


def peers_of(kinds):
    me_c = lax.axis_index("ctx")
    me_d = lax.axis_index("dp")
    n = lax.axis_size("ctx")
    m = lax.axis_size("dp")
    chips = n // 2
    chip = lax.div(me_c, 2)
    core = lax.rem(me_c, 2)
    found = []
    if any("dp" in kind for kind in kinds):
        found += [{"dp": lax.rem(me_d + r, m)} for r in range(1, m)]
    if "swap_ctx" in kinds:
        found += [{"ctx": lax.rem(me_c + r, n)} for r in range(1, n)]
    elif any(kind.endswith("ctx") for kind in kinds):
        found += [{"ctx": 2 * lax.rem(chip + r, chips) + core} for r in range(1, chips)]
        found += [{"ctx": 2 * chip + 1 - core}]
    return found


def send(src, dst, send_sem, recv_sem, device):
    return pltpu.make_async_remote_copy(
        src_ref=src,
        dst_ref=dst,
        send_sem=send_sem,
        recv_sem=recv_sem,
        device_id=device,
        device_id_type=pl.DeviceIdType.MESH,
    )


class GatherDp:
    scratch = 0

    def __init__(self, x, out, sems):
        self.x, self.out, self.sems = x, out, sems
        self.m = lax.axis_size("dp")
        self.me = lax.axis_index("dp")

    def piece(self, to):
        return self.x

    def target(self, of):
        return self.out.at[of]

    def copy(self, r, of, to):
        return send(
            self.piece(to),
            self.target(of),
            self.sems[0].at[r],
            self.sems[1].at[of],
            {"dp": to},
        )

    def start(self):
        self.sent = []
        for r in range(1, self.m):
            copy = self.copy(r, self.me, lax.rem(self.me + r, self.m))
            copy.start()
            self.sent.append(copy)
        self.keep()

    def keep(self):
        self.out[self.me] = self.x[...]

    def middle(self, t):
        pass

    def finish(self):
        for r in range(1, self.m):
            of = lax.rem(self.me + self.m - r, self.m)
            self.copy(r, of, of).wait_recv()
        for copy in self.sent:
            copy.wait_send()


class SwapDp(GatherDp):
    def piece(self, to):
        return self.x.at[to]

    def keep(self):
        self.out[self.me] = self.x[self.me]


class SumDp(SwapDp):
    scratch = 1

    def __init__(self, x, out, sems, got):
        super().__init__(x, out, sems)
        self.got = got

    def target(self, of):
        return self.got.at[of]

    def keep(self):
        pass

    def finish(self):
        super().finish()
        total = self.x[self.me].astype(jnp.float32)
        for r in range(1, self.m):
            total = total + self.got[lax.rem(self.me + r, self.m)].astype(jnp.float32)
        self.out[...] = total


class SwapCtx(SwapDp):
    def __init__(self, x, out, sems):
        self.x, self.out, self.sems = x, out, sems
        self.m = lax.axis_size("ctx")
        self.me = lax.axis_index("ctx")

    def copy(self, r, of, to):
        return send(
            self.piece(to),
            self.target(of),
            self.sems[0].at[r],
            self.sems[1].at[of],
            {"ctx": to},
        )


class Line:
    def setup(self):
        self.chips = lax.axis_size("ctx") // 2
        self.me = lax.axis_index("ctx")
        self.chip = lax.div(self.me, 2)
        self.core = lax.rem(self.me, 2)
        self.partner = 2 * self.chip + 1 - self.core
        self.sent = []

    def launch(self, copy, when=None):
        self.sent.append((copy, when))
        if when is None:
            copy.start()
        else:
            pl.when(when)(copy.start)

    def drain(self):
        for copy, when in self.sent:
            if when is None:
                copy.wait_send()
            else:
                pl.when(when)(copy.wait_send)

    def sides(self):
        return (
            (1, self.chip < self.chips - 1, self.chip > 0),
            (-1, self.chip > 0, self.chip < self.chips - 1),
        )

    def safe(self, chip):
        return lax.min(lax.max(chip, 0), self.chips - 1)


class GatherCtx(Line):
    scratch = 0

    def __init__(self, x, out, sems):
        self.x, self.out, self.sems = x, out, sems
        self.setup()

    def of_chip(self, r, core):
        return 2 * lax.rem(self.chip + self.chips + r, self.chips) + core

    def copy(self, src, slot, of, to):
        return send(
            src, self.out.at[of], self.sems[0].at[slot], self.sems[1].at[of], {"ctx": to}
        )

    def start(self):
        for side, onward, _ in self.sides():
            to = 2 * self.safe(self.chip + side) + self.core
            self.launch(self.copy(self.x, (side + 1) // 2, self.me, to), onward)
        self.launch(self.copy(self.x, 2, self.me, self.partner))
        self.out[self.me] = self.x[...]

    def middle(self, t):
        for side, onward, _ in self.sides():
            chip = self.chip - side * t
            here = (chip >= 0) & (chip < self.chips)
            of = 2 * self.safe(chip) + self.core
            slot = 3 + 4 * (t - 1) + (side + 1)
            pl.when(here)(self.copy(self.x, slot, of, of).wait_recv)
            to = 2 * self.safe(self.chip + side) + self.core
            self.launch(self.copy(self.out.at[of], slot, of, to), here & onward)
            self.launch(self.copy(self.out.at[of], slot + 1, of, self.partner), here)

    def finish(self):
        for r in range(self.chips):
            of = self.of_chip(-r, 1 - self.core)
            self.copy(self.x, 2, of, self.partner).wait_recv()
        self.drain()


class ShrinkGather(Line):
    scratch = 1

    def __init__(self, x, out, sems, line):
        self.x, self.out, self.sems, self.line = x, out, sems, line
        self.setup()
        self.m = lax.axis_size("dp")
        self.row = lax.axis_index("dp")

    def along(self, src, slot, of, to):
        return send(
            src, self.line.at[of], self.sems[0].at[slot], self.sems[1].at[of],
            {"ctx": 2 * to + self.core},
        )

    def across(self, src, slot, of, to):
        return send(
            src, self.out.at[of, self.core], self.sems[0].at[slot],
            self.sems[1].at[self.chips + of], {"dp": to},
        )

    def over(self, slot, of, core):
        return send(
            self.out.at[of, core], self.out.at[of, core], self.sems[0].at[slot],
            self.sems[1].at[self.chips + self.m + of], {"ctx": self.partner},
        )

    def place(self, src, chip, slot, when):
        mine = chip == self.row
        ok = mine if when is None else when & mine

        @pl.when(ok)
        def _():
            self.out[self.row, self.core] = src[...]

        other = chip != self.row
        to = lax.rem(chip + 0 * self.row, self.m)
        self.launch(self.across(src, slot, self.row, to), other if when is None else when & other)

    def start(self):
        for side, onward, _ in self.sides():
            to = self.safe(self.chip + side)
            self.launch(self.along(self.x, (side + 1) // 2, self.chip, to), onward)
        self.place(self.x, self.chip, 2, None)

    def middle(self, t):
        for side, onward, _ in self.sides():
            chip = self.chip - side * t
            here = (chip >= 0) & (chip < self.chips)
            of = self.safe(chip)
            slot = 3 + 4 * (t - 1) + (side + 1)
            pl.when(here)(self.along(self.x, slot, of, of).wait_recv)
            to = self.safe(self.chip + side)
            self.launch(self.along(self.line.at[of], slot, of, to), here & onward)
            self.place(self.line.at[of], of, slot + 1, here)

    def finish(self):
        base = 3 + 4 * (self.chips - 1)
        self.launch(self.over(base, self.row, self.core))
        for r in range(1, self.m):
            of = lax.rem(self.row + r, self.m)
            self.across(self.x, 2, of, of).wait_recv()
            self.launch(self.over(base + r, of, self.core))
        for of in range(self.m):
            self.over(base, of, 1 - self.core).wait_recv()
        self.drain()


class SumCtx(Line):
    scratch = 3

    def __init__(self, x, out, sems, half, pre, got):
        self.x, self.out, self.sems = x, out, sems
        self.half, self.pre, self.got = half, pre, got
        self.setup()

    def early(self, r):
        j = lax.rem(self.chip + r, self.chips)
        return send(
            self.x.at[2 * j + 1 - self.core],
            self.half.at[j],
            self.sems[0].at[r],
            self.sems[1].at[j],
            {"ctx": self.partner},
        )

    def late(self, r, of, to):
        return send(
            self.pre.at[to],
            self.got.at[of],
            self.sems[0].at[self.chips + r],
            self.sems[1].at[self.chips + of],
            {"ctx": 2 * to + self.core},
        )

    def start(self):
        for r in list(range(1, self.chips)) + [0]:
            self.launch(self.early(r))

    def middle(self, r):
        self.early(r).wait_recv()
        to = lax.rem(self.chip + r, self.chips)
        total = self.x[2 * to + self.core].astype(jnp.float32) + self.half[to].astype(jnp.float32)
        self.pre[to] = total.astype(self.pre.dtype)
        self.launch(self.late(r, self.chip, to))

    def finish(self):
        self.early(0).wait_recv()
        total = self.x[self.me].astype(jnp.float32) + self.half[self.chip].astype(jnp.float32)
        for r in range(1, self.chips):
            of = lax.rem(self.chip + self.chips - r, self.chips)
            self.late(r, of, of).wait_recv()
            total = total + self.got[of].astype(jnp.float32)
        self.out[...] = total
        self.drain()


class ShrinkCross(Line):
    scratch = 2

    def __init__(self, x, out, sems, half, pre):
        self.x, self.out, self.sems = x, out, sems
        self.half, self.pre = half, pre
        self.setup()
        self.m = lax.axis_size("dp")
        self.row = lax.axis_index("dp")

    def early(self, r):
        j = lax.rem(self.row + r, self.m)
        return send(
            self.x.at[j, 1 - self.core],
            self.half.at[j],
            self.sems[0].at[r],
            self.sems[1].at[j],
            {"ctx": self.partner},
        )

    def across(self, r, of, to):
        return send(
            self.pre.at[to],
            self.out.at[of],
            self.sems[0].at[self.m + r],
            self.sems[1].at[self.m + of],
            {"dp": to},
        )

    def add(self, j):
        total = self.x[j, self.core].astype(jnp.float32) + self.half[j].astype(jnp.float32)
        return total.astype(self.pre.dtype)

    def start(self):
        for r in list(range(1, self.m)) + [0]:
            self.launch(self.early(r))

    def middle(self, r):
        self.early(r).wait_recv()
        to = lax.rem(self.row + r, self.m)
        self.pre[to] = self.add(to)
        self.launch(self.across(r, self.row, to))

    def finish(self):
        self.early(0).wait_recv()
        self.out[self.row] = self.add(self.row)
        for r in range(1, self.m):
            of = lax.rem(self.row + self.m - r, self.m)
            self.across(r, of, of).wait_recv()
        self.drain()


class LineSum(Line):
    scratch = 1

    def __init__(self, x, out, sems, got):
        self.x, self.out, self.sems, self.got = x, out, sems, got
        self.setup()

    def along(self, r, of, to):
        return send(
            self.x.at[to],
            self.got.at[of],
            self.sems[0].at[r],
            self.sems[1].at[of],
            {"ctx": 2 * to + self.core},
        )

    def start(self):
        for r in range(1, self.chips):
            self.launch(self.along(r, self.chip, lax.rem(self.chip + r, self.chips)))

    def middle(self, t):
        pass

    def finish(self):
        total = self.x[self.chip].astype(jnp.float32)
        for r in range(1, self.chips):
            of = lax.rem(self.chip + self.chips - r, self.chips)
            self.along(r, of, of).wait_recv()
            total = total + self.got[of].astype(jnp.float32)
        self.out[...] = total
        self.drain()


class HalfGather(Line):
    scratch = 0

    def __init__(self, x, out, sems):
        self.x, self.out, self.sems = x, out, sems
        self.setup()
        self.m = lax.axis_size("dp")
        self.row = lax.axis_index("dp")

    def across(self, r, of, to):
        return send(
            self.x.at[self.core],
            self.out.at[of, self.core],
            self.sems[0].at[r],
            self.sems[1].at[of],
            {"dp": to},
        )

    def over(self, r, of, core):
        return send(
            self.out.at[of, core],
            self.out.at[of, core],
            self.sems[0].at[self.m + r],
            self.sems[1].at[self.m + of],
            {"ctx": self.partner},
        )

    def start(self):
        for r in range(1, self.m):
            self.launch(self.across(r, self.row, lax.rem(self.row + r, self.m)))
        self.out[self.row] = self.x[...]

    def middle(self, r):
        of = lax.rem(self.row + self.m - r, self.m)
        self.across(r, of, of).wait_recv()
        self.launch(self.over(r, of, self.core))

    def finish(self):
        for r in range(1, self.m):
            self.over(r, lax.rem(self.row + r, self.m), 1 - self.core).wait_recv()
        self.drain()


MOVES = {
    "gather_dp": GatherDp,
    "swap_dp": SwapDp,
    "sum_dp": SumDp,
    "gather_ctx": GatherCtx,
    "swap_ctx": SwapCtx,
    "sum_ctx": SumCtx,
    "shrink_gather_dp_ctx": ShrinkGather,
    "shrink_cross_dp_ctx": ShrinkCross,
    "line_sum_ctx": LineSum,
    "half_gather_dp_ctx": HalfGather,
}


def move_kernel(kinds, *refs):
    count = len(kinds)
    xs, outs, rest = refs[:count], refs[count : 2 * count], list(refs[2 * count :])
    barrier = pltpu.get_barrier_semaphore()
    peers = peers_of(kinds)
    for peer in peers:
        pl.semaphore_signal(
            barrier, inc=1, device_id=peer, device_id_type=pl.DeviceIdType.MESH
        )
    pl.semaphore_wait(barrier, len(peers))
    moves = []
    for kind, x, out in zip(kinds, xs, outs):
        sems = (rest.pop(0), rest.pop(0))
        extra = [rest.pop(0) for _ in range(MOVES[kind].scratch)]
        moves.append(MOVES[kind](x, out, sems, *extra))
    for move in moves:
        move.start()
    for t in range(1, lax.axis_size("ctx") // 2):
        for move in moves:
            move.middle(t)
    for move in moves:
        move.finish()


def move(collective_id, *pairs):
    kinds = tuple(kind for kind, _ in pairs)
    n = lax.axis_size("ctx")
    m = lax.axis_size("dp")
    shapes, scratch, sent = [], [], 0
    for kind, x in pairs:
        size = n if kind.endswith("ctx") else m
        one = x.dtype
        semaphores = size
        sent += x.size * x.dtype.itemsize
        extra = []
        if kind == "shrink_gather_dp_ctx":
            shape = jax.ShapeDtypeStruct((m, 2) + x.shape, one)
            extra = [pltpu.VMEM((n // 2,) + x.shape, one)]
            semaphores = 2 * n + m
        elif kind == "shrink_cross_dp_ctx":
            shape = jax.ShapeDtypeStruct((m,) + x.shape[2:], one)
            extra = [pltpu.VMEM((m,) + x.shape[2:], one)] * 2
            semaphores = 2 * m
        elif kind == "line_sum_ctx":
            shape = jax.ShapeDtypeStruct(x.shape[1:], jnp.float32)
            extra = [pltpu.VMEM(x.shape, one)]
        elif kind == "half_gather_dp_ctx":
            shape = jax.ShapeDtypeStruct((m,) + x.shape, one)
            semaphores = 2 * m
        elif kind.startswith("gather"):
            shape = jax.ShapeDtypeStruct((size,) + x.shape, one)
            semaphores = 2 * size
        elif kind.startswith("swap"):
            shape = jax.ShapeDtypeStruct(x.shape, one)
        else:
            shape = jax.ShapeDtypeStruct(x.shape[1:], jnp.float32)
            if kind == "sum_dp":
                extra = [pltpu.VMEM(x.shape, one)]
            else:
                extra = [pltpu.VMEM((n // 2,) + x.shape[1:], one)] * 3
        shapes.append(shape)
        scratch += [pltpu.SemaphoreType.DMA((semaphores,))] * 2 + extra
    kernel = lambda *refs: move_kernel(kinds, *refs)
    return pl.pallas_call(
        kernel,
        in_specs=[pl.BlockSpec(memory_space=pltpu.VMEM)] * len(kinds),
        out_specs=[pl.BlockSpec(memory_space=pltpu.VMEM)] * len(kinds),
        out_shape=shapes,
        scratch_shapes=scratch,
        compiler_params=pltpu.CompilerParams(
            collective_id=collective_id, has_side_effects=True
        ),
        cost_estimate=pl.CostEstimate(flops=sent * 100, bytes_accessed=sent, transcendentals=0),
        name="move_" + str(collective_id),
    )(*[x for _, x in pairs])


def pair_lanes(shape, half):
    lane = lax.broadcasted_iota(jnp.int32, shape, 1)
    return (lane < HD) if half == 0 else (lane >= HD)


def causal(shape):
    row = lax.broadcasted_iota(jnp.int32, shape, 0)
    return row >= lax.broadcasted_iota(jnp.int32, shape, 1)


def sort_rows(order_ref, src, dst, lane):
    for b in range(src.shape[0] // BLK):
        start = pl.multiple_of(order_ref[b] * BLK, BLK)
        dst[b * BLK : (b + 1) * BLK, lane : lane + src.shape[1]] = src[pl.ds(start, BLK), :]


def unsort_rows(order_ref, src, dst, lane):
    for b in range(dst.shape[0] // BLK):
        start = pl.multiple_of(order_ref[b] * BLK, BLK)
        dst[pl.ds(start, BLK), :] = src[b * BLK : (b + 1) * BLK, lane : lane + dst.shape[1]]


def head_slots():
    return ((0, 0), (0, 1), (1, 0))


def pairs_forward(order_ref, main_ref, last_ref, out_ref, log_ref, rows, outs):
    sort_rows(order_ref, main_ref, rows, 0)
    sort_rows(order_ref, last_ref, rows, 3 * TILE)
    seq = main_ref.shape[0]
    step = min(4 * BLK, seq)
    for i in range(seq // step):
        at = slice(i * step, (i + 1) * step)
        results, logs = [], []
        for block, half in head_slots():
            lanes = lambda part: slice((3 * block + part) * TILE, (3 * block + part + 1) * TILE)
            query = rows[at, lanes(0)] * HD ** (-0.5)
            query = query.astype(jnp.bfloat16)
            if block == 0:
                query = jnp.where(pair_lanes(query.shape, half), query, jnp.zeros_like(query))
            last = dot_on(query, rows[at, lanes(1)], 1, 1)
            last = jnp.where(causal(last.shape), last, masked_score)
            top = jnp.max(last, axis=1, keepdims=True)
            if i > 0:
                early = dot_on(query, rows[: i * step, lanes(1)], 1, 1)
                top = jnp.maximum(top, jnp.max(early, axis=1, keepdims=True))
            last = jnp.exp(last - top)
            total = jnp.sum(last, axis=1, keepdims=True)
            if i > 0:
                early = jnp.exp(early - top)
                total = total + jnp.sum(early, axis=1, keepdims=True)
            scale = 1.0 / total
            result = dot_on((last * scale).astype(jnp.bfloat16), rows[at, lanes(2)], 1, 0)
            if i > 0:
                result = result + dot_on(
                    (early * scale).astype(jnp.bfloat16), rows[: i * step, lanes(2)], 1, 0
                )
            results.append(result)
            logs.append(top + jnp.log(total))
        first = pair_lanes((step, TILE), 0)
        outs[at, :TILE] = jnp.where(first, results[0], results[1]).astype(jnp.bfloat16)
        outs[at, TILE:] = results[2].astype(jnp.bfloat16)
        lane = lax.broadcasted_iota(jnp.int32, (step, TILE), 1)
        log_ref[at, :] = jnp.where(lane == 0, logs[0], jnp.where(lane == 1, logs[1], logs[2]))
    unsort_rows(order_ref, outs, out_ref, 0)


def pairs_backward(
    order_ref,
    main_ref,
    last_ref,
    out_ref,
    log_ref,
    dout_ref,
    dmain_ref,
    dlast_ref,
    rows,
    outs,
    douts,
    grads,
    dkey,
    dvalue,
):
    sort_rows(order_ref, main_ref, rows, 0)
    sort_rows(order_ref, last_ref, rows, 3 * TILE)
    sort_rows(order_ref, out_ref, outs, 0)
    sort_rows(order_ref, dout_ref, douts, 0)
    seq = main_ref.shape[0]
    step = min(4 * BLK, seq)
    dkey[...] = jnp.zeros_like(dkey)
    dvalue[...] = jnp.zeros_like(dvalue)
    for i in range(seq // step):
        at = slice(i * step, (i + 1) * step)
        dqueries = []
        for slot, (block, half) in enumerate(head_slots()):
            lanes = lambda part: slice((3 * block + part) * TILE, (3 * block + part + 1) * TILE)
            own = slice(block * TILE, (block + 1) * TILE)
            query = (rows[at, lanes(0)] * HD ** (-0.5)).astype(jnp.bfloat16)
            dout = douts[at, own]
            if block == 0:
                mask = pair_lanes(query.shape, half)
                query = jnp.where(mask, query, jnp.zeros_like(query))
                dout = jnp.where(mask, dout, jnp.zeros_like(dout))
            delta = jnp.sum(
                dout.astype(jnp.float32) * outs[at, own].astype(jnp.float32), axis=1, keepdims=True
            )
            log_total = log_ref[at, slot : slot + 1]
            dquery = None
            for keys, diagonal in ((at, True), (slice(0, i * step), False)):
                if keys.stop == 0:
                    continue
                scores = dot_on(query, rows[keys, lanes(1)], 1, 1)
                probs = jnp.exp(scores - log_total)
                if diagonal:
                    probs = jnp.where(causal(probs.shape), probs, 0.0)
                dprobs = dot_on(dout, rows[keys, lanes(2)], 1, 1)
                dscores = (probs * (dprobs - delta)).astype(jnp.bfloat16)
                part = dot_on(dscores, rows[keys, lanes(1)], 1, 0)
                dquery = part if dquery is None else dquery + part
                dkey[own, keys] += dot_on(query, dscores, 0, 0)
                dvalue[own, keys] += dot_on(dout, probs.astype(jnp.bfloat16), 0, 0)
            dqueries.append(dquery * HD ** (-0.5))
        first = pair_lanes((step, TILE), 0)
        grads[at, :TILE] = jnp.where(first, dqueries[0], dqueries[1]).astype(jnp.bfloat16)
        third = jnp.where(first, dqueries[2], 0.0)
        grads[at, 3 * TILE : 4 * TILE] = third.astype(jnp.bfloat16)
    for block in range(2):
        own = slice(block * TILE, (block + 1) * TILE)
        grads[:, (3 * block + 1) * TILE : (3 * block + 2) * TILE] = dkey[own, :].T.astype(jnp.bfloat16)
        grads[:, (3 * block + 2) * TILE : (3 * block + 3) * TILE] = dvalue[own, :].T.astype(jnp.bfloat16)
    unsort_rows(order_ref, grads, dmain_ref, 0)
    unsort_rows(order_ref, grads, dlast_ref, 3 * TILE)


def attend(kernel, order, arrays, shapes, scratch, matmuls):
    seq = arrays[0].shape[0]
    vmem = pl.BlockSpec(memory_space=pltpu.VMEM)
    return pl.pallas_call(
        kernel,
        in_specs=[pl.BlockSpec(memory_space=pltpu.SMEM)] + [vmem] * len(arrays),
        out_specs=[vmem] * len(shapes),
        out_shape=shapes,
        scratch_shapes=scratch,
        cost_estimate=pl.CostEstimate(
            flops=3 * matmuls * seq * seq * TILE,
            bytes_accessed=seq * 24 * TILE,
            transcendentals=2 * seq * seq,
        ),
    )(order, *arrays)


def trade(x):
    return lax.ppermute(x, "ctx", [(c, c ^ 1) for c in range(lax.axis_size("ctx"))])


def core_pair(mine, other, axis):
    first = lax.axis_index("ctx") % 2 == 0
    return jnp.where(
        first, jnp.concatenate([mine, other], axis), jnp.concatenate([other, mine], axis)
    )


def local_pairs(
    inputs,
    out_grad,
    pair_blocks,
    triple_weight,
    merge_weight,
    expand_weight,
    shrink_weight,
    vector_params,
    triple_moment,
    merge_moment,
    expand_moment,
    shrink_moment,
    vector_moment,
    triple_square,
    merge_square,
    expand_square,
    shrink_square,
    vector_square,
):
    bf16 = jnp.bfloat16
    f32 = jnp.float32
    n = lax.axis_size("ctx")
    m = lax.axis_size("dp")
    here = lax.axis_index("ctx")
    seq_here = lax.axis_index("dp")
    rows = inputs.shape[1]
    total = rows * n
    feat = D // n
    cut = n * TILE
    spare = D - cut
    wide = expand_weight.shape[1]
    hid = shrink_weight.shape[0]
    fold = wide // hid
    cols = shrink_weight.shape[1]
    stream = inputs[0]
    cotangent = out_grad[0]
    tw, mw = triple_weight.shape[1], merge_weight.shape[1]

    flat = pair_blocks.reshape(-1)
    blocks = jnp.arange(flat.shape[0], dtype=jnp.int32)
    order = jnp.sum(jnp.where(flat[None, :] == blocks[:, None], blocks[None, :], 0), axis=1)

    w_expand_own = expand_weight.astype(bf16)
    first_core = here % 2 == 0
    shrink_t = shrink_weight.astype(bf16).T
    upper, lower = shrink_t[: cols // fold], shrink_t[cols // fold :]
    w_shrink_own = core_pair(
        jnp.where(first_core, upper, lower), trade(jnp.where(first_core, lower, upper)), 1
    )
    packed = jnp.concatenate(
        [triple_weight.astype(bf16), vector_params.astype(bf16)], axis=1
    )
    normed_one, inverse_one = layer_norm(stream)
    cot_b = cotangent.astype(bf16)
    normed_full, merge_line, columns, cot_full = move(
        0,
        ("gather_ctx", normed_one.astype(bf16)),
        ("gather_ctx", merge_weight.astype(bf16)),
        ("gather_dp", packed),
        ("gather_dp", cot_b),
    )
    normed_full = normed_full.reshape(total, D)
    cot_full = cot_full.reshape(m * rows, D)

    def take(start, width):
        return columns[:, :, start : start + width].transpose(1, 0, 2).reshape(feat, m * width)

    triple_rows = take(0, tw).reshape(feat, 3, D)
    vector_rows = take(tw, vector_params.shape[1])
    slabs = (
        triple_rows[:, :, :cut].reshape(feat, 3, n, TILE).transpose(2, 0, 1, 3).reshape(n, feat, -1)
    )
    common = jnp.concatenate([triple_rows[:, :, cut:].reshape(feat, 3 * spare), vector_rows], axis=1)
    w_main, w_common, w_merge, w_shrink_t = move(
        1,
        ("swap_ctx", slabs),
        ("gather_ctx", common),
        ("half_gather_dp_ctx", merge_line.reshape(2, D // 2, mw)),
        ("shrink_gather_dp_ctx", w_shrink_own),
    )
    w_shrink_t = w_shrink_t.reshape(D, wide)
    w_merge = w_merge.reshape(m, D, mw).transpose(1, 0, 2).reshape(D, D)
    w_main = w_main.reshape(D, 3 * TILE)
    w_common = w_common.reshape(D, -1)
    near = lax.broadcasted_iota(jnp.int32, (w_common.shape[1], 3 * TILE), 0)
    far = lax.broadcasted_iota(jnp.int32, (w_common.shape[1], 3 * TILE), 1)
    spread = (far % TILE < spare) & (near == far // TILE * spare + far % TILE)
    w_last = dot_on(w_common, spread.astype(bf16), 1, 0).astype(bf16)
    vectors = w_common[:, 3 * spare :].astype(f32)
    gain_one = vectors[:, 0]
    shift_one = vectors[:, 1]
    merge_bias = vectors[:, 4]
    gain_two = vectors[:, 5]
    shift_two = vectors[:, 6]
    shrink_bias = vectors[:, 7]
    expand_bias = lax.dynamic_slice_in_dim(vectors[:, 8:].T.reshape(-1), seq_here * wide, wide)

    def main_bias(column):
        return lax.dynamic_slice_in_dim(vectors[:, column], here * TILE, TILE)

    def last_bias(column):
        return jnp.pad(vectors[cut:, column], (0, TILE - spare))

    zeros = jnp.zeros((TILE,), f32)
    bias_main = jnp.concatenate([main_bias(2), zeros, main_bias(3)])
    bias_last = jnp.concatenate([last_bias(2), zeros, last_bias(3)])
    act_one = (normed_full.astype(f32) * gain_one + shift_one).astype(bf16)
    qkv_main = (dot_on(act_one, w_main, 1, 0) + bias_main).astype(bf16)
    qkv_last = (dot_on(act_one, w_last, 1, 0) + bias_last).astype(bf16)
    rows_scratch = pltpu.VMEM((total, 6 * TILE), bf16)
    half_scratch = pltpu.VMEM((total, 2 * TILE), bf16)
    attended, log_total = attend(
        pairs_forward,
        order,
        (qkv_main, qkv_last),
        [
            jax.ShapeDtypeStruct((total, 2 * TILE), bf16),
            jax.ShapeDtypeStruct((total, TILE), f32),
        ],
        [rows_scratch, half_scratch],
        2,
    )
    (att_main,) = move(2, ("swap_ctx", attended[:, :TILE].reshape(n, rows, TILE)))
    att_last = lax.dynamic_slice(attended, (here * rows, TILE), (rows, spare))
    att_own = jnp.concatenate(
        [att_main.transpose(1, 0, 2).reshape(rows, cut), att_last], axis=1
    )
    middle = stream + dot_on(att_own, w_merge, 1, 0) + merge_bias
    normed_two, inverse_two = layer_norm(middle)
    act_two, w_expand = move(
        3,
        ("gather_dp", (normed_two * gain_two + shift_two).astype(bf16)),
        ("gather_ctx", w_expand_own),
    )
    w_expand = w_expand.reshape(D, wide)
    act_two = act_two.reshape(m * rows, D)
    pre_act = dot_on(act_two, w_expand, 1, 0) + expand_bias
    hidden_b = gelu_value(pre_act).astype(bf16)
    dpre = dot_on(cot_full, w_shrink_t, 1, 0) * gelu_slope(pre_act)
    dpre_b = dpre.astype(bf16)
    expand_bias_grad = jnp.sum(dpre, axis=0)
    dact_part = dot_on(dpre_b, w_expand, 1, 1).astype(bf16).reshape(m, rows, D)
    expand_part = dot_on(act_two, dpre_b, 0, 0).astype(bf16).reshape(n, feat, wide)
    dact_two, expand_grad = move(4, ("sum_dp", dact_part), ("sum_ctx", expand_part))
    out_part = dot_on(hidden_b, w_shrink_t, 1, 1).astype(bf16).reshape(m, rows, D)

    shrink_part = (
        dot_on(cot_full, hidden_b, 0, 0).astype(bf16).reshape(m, fold, cols // fold, wide)
    )

    shrink_bias_grad = jnp.sum(cotangent, axis=0)
    gain_two_grad = jnp.sum(dact_two * normed_two, axis=0)
    shift_two_grad = jnp.sum(dact_two, axis=0)
    dmiddle = cotangent + norm_back(dact_two, normed_two, inverse_two, gain_two)
    dmiddle_b = dmiddle.astype(bf16)
    merge_bias_grad = jnp.sum(dmiddle, axis=0)
    dattended = dot_on(dmiddle_b, w_merge, 1, 1).astype(bf16)
    merge_part = dot_on(att_own, dmiddle_b, 0, 0).astype(bf16).reshape(n, feat, D)
    datt_main, datt_last, merge_rows_grad = move(
        5,
        ("swap_ctx", dattended[:, :cut].reshape(rows, n, TILE).transpose(1, 0, 2)),
        ("gather_ctx", jnp.pad(dattended[:, cut:], ((0, 0), (0, TILE - spare)))),
        ("sum_ctx", merge_part),
    )
    datt = jnp.concatenate(
        [datt_main.reshape(total, TILE), datt_last.reshape(total, TILE)], axis=1
    )
    dqkv_main, dqkv_last = attend(
        pairs_backward,
        order,
        (qkv_main, qkv_last, attended, log_total, datt),
        [jax.ShapeDtypeStruct((total, 3 * TILE), bf16)] * 2,
        [
            rows_scratch,
            half_scratch,
            half_scratch,
            rows_scratch,
            pltpu.VMEM((2 * TILE, total), f32),
            pltpu.VMEM((2 * TILE, total), f32),
        ],
        5,
    )
    counted = here == 0
    dqkv_counted = jnp.where(counted, dqkv_last, jnp.zeros_like(dqkv_last))
    dact_part = dot_on(dqkv_main, w_main, 1, 1) + dot_on(dqkv_counted, w_last, 1, 1)
    dact_part = dact_part.astype(bf16).reshape(n, rows, D)
    dact_one, shrink_cross = move(
        6, ("sum_ctx", dact_part), ("shrink_cross_dp_ctx", shrink_part)
    )
    bias_grads = jnp.concatenate(
        [jnp.sum(dqkv_main.astype(f32), axis=0), jnp.sum(dqkv_counted.astype(f32), axis=0)]
    )
    gain_one_grad = jnp.sum(dact_one * normed_one, axis=0)
    shift_one_grad = jnp.sum(dact_one, axis=0)
    input_rows = dmiddle + norm_back(dact_one, normed_one, inverse_one, gain_one)

    def place(part):
        main = lax.dynamic_update_slice_in_dim(
            jnp.zeros((cut,), f32), bias_grads[part * TILE :][:TILE], here * TILE, 0
        )
        return jnp.concatenate([main, bias_grads[(3 + part) * TILE :][:spare]])

    expand_bias_all = lax.dynamic_update_slice_in_dim(
        jnp.zeros((m * wide,), f32), expand_bias_grad, seq_here * wide, 0
    )
    vector_local = jnp.concatenate(
        [
            jnp.stack(
                [
                    gain_one_grad,
                    shift_one_grad,
                    place(0),
                    place(2),
                    merge_bias_grad,
                    gain_two_grad,
                    shift_two_grad,
                    shrink_bias_grad,
                ],
                axis=1,
            ),
            expand_bias_all.reshape(-1, D).T,
        ],
        axis=1,
    )
    triple_part = dot_on(act_one, dqkv_main, 0, 0).astype(bf16).reshape(n, feat, 3 * TILE)
    triple_last = dot_on(act_one, dqkv_last, 0, 0).astype(bf16)
    triple_main, vector_rows_grad, out_sum = move(
        7,
        ("swap_ctx", triple_part),
        ("sum_ctx", vector_local.reshape(n, feat, -1)),
        ("sum_dp", out_part),
    )
    triple_last = lax.dynamic_slice_in_dim(triple_last, here * feat, feat, 0)
    triple_last = triple_last.reshape(feat, 3, TILE)[:, :, :spare]
    triple_rows_grad = jnp.concatenate(
        [
            triple_main.reshape(n, feat, 3, TILE).transpose(1, 2, 0, 3).reshape(feat, 3, cut),
            triple_last,
        ],
        axis=2,
    )

    block_out = middle + out_sum + shrink_bias

    def by_dp(rows_part):
        return rows_part.reshape(feat, m, -1).transpose(1, 0, 2).astype(bf16)

    last, shrink_sum = move(
        8,
        (
            "sum_dp",
            jnp.concatenate(
                [by_dp(triple_rows_grad), by_dp(merge_rows_grad), by_dp(vector_rows_grad)], axis=2
            ),
        ),
        ("line_sum_ctx", shrink_cross),
    )
    left, right = shrink_sum[:, :hid], shrink_sum[:, hid:]
    shrink_grad = core_pair(
        jnp.where(first_core, left, right), trade(jnp.where(first_core, right, left)), 0
    ).T
    triple_grad = last[:, :tw]
    merge_grad = last[:, tw : tw + mw]
    vector_grad = last[:, tw + mw :]
    triple_new, triple_moment_new, triple_square_new = adam_update(
        triple_weight, triple_grad, triple_moment, triple_square, True
    )
    merge_new, merge_moment_new, merge_square_new = adam_update(
        merge_weight, merge_grad, merge_moment, merge_square, True
    )
    expand_new, expand_moment_new, expand_square_new = adam_update(
        expand_weight, expand_grad, expand_moment, expand_square, True
    )
    shrink_new, shrink_moment_new, shrink_square_new = adam_update(
        shrink_weight, shrink_grad, shrink_moment, shrink_square, True
    )
    vector_new, vector_moment_new, vector_square_new = adam_update(
        vector_params, vector_grad, vector_moment, vector_square, False
    )
    return (
        block_out[None],
        input_rows[None],
        triple_grad,
        merge_grad,
        expand_grad,
        shrink_grad,
        vector_grad,
        triple_new,
        merge_new,
        expand_new,
        shrink_new,
        vector_new,
        triple_moment_new,
        merge_moment_new,
        expand_moment_new,
        shrink_moment_new,
        vector_moment_new,
        triple_square_new,
        merge_square_new,
        expand_square_new,
        shrink_square_new,
        vector_square_new,
    )


def solution(mesh):
    heads = H // 2
    even = mesh.shape["ctx"] == heads == 2 * mesh.shape["dp"]
    local = local_pairs if even else local_wide
    in_specs = (
        P("dp", "ctx", None),
        P("dp", "ctx", None),
        P(),
        P("ctx", "dp"),
        P("ctx", "dp"),
        P("ctx", "dp"),
        P("ctx", "dp"),
        P("ctx", "dp"),
        P("ctx", "dp"),
        P("ctx", "dp"),
        P("ctx", "dp"),
        P("ctx", "dp"),
        P("ctx", "dp"),
        P("ctx", "dp"),
        P("ctx", "dp"),
        P("ctx", "dp"),
        P("ctx", "dp"),
        P("ctx", "dp"),
    )
    out_specs = (
        P("dp", "ctx", None),
        P("dp", "ctx", None),
        P("ctx", "dp"),
        P("ctx", "dp"),
        P("ctx", "dp"),
        P("ctx", "dp"),
        P("ctx", "dp"),
        P("ctx", "dp"),
        P("ctx", "dp"),
        P("ctx", "dp"),
        P("ctx", "dp"),
        P("ctx", "dp"),
        P("ctx", "dp"),
        P("ctx", "dp"),
        P("ctx", "dp"),
        P("ctx", "dp"),
        P("ctx", "dp"),
        P("ctx", "dp"),
        P("ctx", "dp"),
        P("ctx", "dp"),
        P("ctx", "dp"),
        P("ctx", "dp"),
    )
    return jax.shard_map(local, mesh=mesh, in_specs=in_specs, out_specs=out_specs, check_vma=False)
```
